32 devices in a mesh: img: 8 (over z, x), seq: 4 (over y, core).
Axes of the slice: x: 2, y: 2, z: 4, core: 2. Of those that a mesh axis runs over, the one named last changes fastest.
Arguments:
- tokens: bfloat16 [4864, 1024], P(('img', 'seq')), may hold values from -6 to 6
- classes: int32 [32], P('img'), may hold values 0 or 1
- source_index: int32 [145, 4], replicated, may hold values from 0 to 49
- position_table: float32 [50, 1024], replicated, may hold values from -3 to 3
- input_weight: bfloat16 [1024, 3072], P('img'), may hold values from -0.1875 to 0.1875
- query_bias: float32 [1024], replicated, may hold values from -3 to 3
- value_bias: float32 [1024], replicated, may hold values from -3 to 3
- output_weight: bfloat16 [1024, 1024], P('img'), may hold values from -0.75 to 0.75
- output_bias: float32 [1024], replicated, may hold values from -2 to 2
- up_weight: bfloat16 [1024, 4096], P('img'), may hold values from -0.1875 to 0.1875
- up_bias: float32 [4096], replicated, may hold values from -3 to 3
- down_weight: bfloat16 [4096, 1024], P('img'), may hold values from -0.09375 to 0.09375
- down_bias: float32 [1024], replicated, may hold values from -2 to 2
- first_gain: float32 [1024], replicated, may hold values from 0.5 to 1.5
- first_shift: float32 [1024], replicated, may hold values from -2 to 2
- second_gain: float32 [1024], replicated, may hold values from 0.5 to 1.5
- second_shift: float32 [1024], replicated, may hold values from -2 to 2
- cotangent: bfloat16 [4864, 1024], P(('img', 'seq')), may hold values from -6 to 6
Outputs:
- block_out: bfloat16 [4864, 1024], P(('img', 'seq'))
- tokens_grad: bfloat16 [4864, 1024], P(('img', 'seq'))
- position_grad: float32 [50, 1024], replicated
- input_weight_grad: float32 [1024, 3072], P('img')
- query_bias_grad: float32 [1024], replicated
- value_bias_grad: float32 [1024], replicated
- output_weight_grad: float32 [1024, 1024], P('img')
- output_bias_grad: float32 [1024], replicated
- up_weight_grad: float32 [1024, 4096], P('img')
- up_bias_grad: float32 [4096], replicated
- down_weight_grad: float32 [4096, 1024], P('img')
- down_bias_grad: float32 [1024], replicated
- first_gain_grad: float32 [1024], replicated
- first_shift_grad: float32 [1024], replicated
- second_gain_grad: float32 [1024], replicated
- second_shift_grad: float32 [1024], replicated
The draws below stay inside these ranges and needn't reach their ends.
Inputs may be any that keep to these rules, and one draw needn't show every extreme that they name: `classes`: 0 marks an image of 50 tokens, 1 an image of 145 tokens; the 4 images of one index of img fill its slots end to end in order, the rest being padding.
All inputs are finite; a program needn't handle non-finite values. No bound on the sum of `classes` on one device may be relied on, other than what follows from the above.
Results may differ from the reference program's by a relative error of at most 0.013.
Values may be sent and summed in bfloat16 or wider, within the bound.
No kernel may reach another device: no remote copies, remote signals or barrier semaphores. Data moves between devices by JAX's collectives and lax.ppermute only.
A program may use at most 192 MiB of HBM per device.

```python
import jax
import jax.numpy as jnp
from jax import lax

D = 1024
HEADS = 16
HEAD_DIM = 64
FF = 4096
TABLE = 50
LONG = 145
IMG_GRP = 4
GRP_SLOTS = 608
TOKENS = 4864
IMAGES = 32
N_IMG = 8


def plant(result, rng, least, top_value):
    spot = [jax.random.randint(jax.random.fold_in(rng, axis), (), 0, length) for axis, length in enumerate(result.shape)]
    main_axis = result.shape.index(max(result.shape))
    beside = spot[:main_axis] + [(spot[main_axis] + 1) % result.shape[main_axis]] + spot[main_axis + 1:]
    return result.at[tuple(spot)].set(least).at[tuple(beside)].set(top_value)


def shard_levels(own_key, shape, cuts, low, high):
    factor_of, own = 1.0, jax.random.fold_in(own_key, 6)
    for position, parts in cuts:
        steps = jnp.exp(jax.random.uniform(jax.random.fold_in(own, position), (parts,), jnp.float32, low / len(cuts), high / len(cuts)))
        factor_of = factor_of * jnp.repeat(steps, shape[position] // parts).reshape([-1 if axis == position else 1 for axis in range(len(shape))])
    return factor_of


def bell_draw(key, shape, deviation, bound, shards=(), kind=jnp.bfloat16):
    gain = shard_levels(key, shape, shards, -0.22, 0.18) if shards else 1.0
    entries = jax.random.normal(key, shape, jnp.float32) * deviation * gain
    return jnp.minimum(jnp.maximum(entries, -bound), bound).astype(kind)


def setup_inputs(seed: int = 0) -> dict:
    splits = jax.random.split(jax.random.key(seed), 19)
    return {
        "tokens": bell_draw(splits[0], (TOKENS, D), 1.0, 6.0, ((0, 32),)),
        "classes": plant((jax.random.randint(splits[1], (IMAGES,), 0, 7) < 2).astype(jnp.int32), jax.random.fold_in(splits[1], 1), 0, 1),
        "source_index": plant(jax.random.randint(splits[2], (LONG, 4), 0, TABLE), jax.random.fold_in(splits[2], 1), 0, TABLE - 1).astype(jnp.int32),
        "position_table": bell_draw(splits[3], (TABLE, D), 0.5, 3.0, (), jnp.float32),
        "input_weight": bell_draw(splits[4], (D, 3 * D), D ** -0.5, 0.1875, ((0, 8),)),
        "query_bias": bell_draw(splits[5], (D,), 0.5, 3.0, (), jnp.float32),
        "value_bias": bell_draw(splits[6], (D,), 0.5, 3.0, (), jnp.float32),
        "output_weight": bell_draw(splits[7], (D, D), (D // 16) ** -0.5, 0.75, ((0, 8),)),
        "output_bias": bell_draw(splits[8], (D,), 0.3, 2.0, (), jnp.float32),
        "up_weight": bell_draw(splits[9], (D, FF), D ** -0.5, 0.1875, ((0, 8),)),
        "up_bias": bell_draw(splits[10], (FF,), 0.5, 3.0, (), jnp.float32),
        "down_weight": bell_draw(splits[11], (FF, D), FF ** -0.5, 0.09375, ((0, 8),)),
        "down_bias": bell_draw(splits[12], (D,), 0.3, 2.0, (), jnp.float32),
        "first_gain": jnp.clip(1.0 + 0.1 * jax.random.normal(splits[13], (D,), jnp.float32), 0.5, 1.5),
        "first_shift": bell_draw(splits[14], (D,), 0.3, 2.0, (), jnp.float32),
        "second_gain": jnp.clip(1.0 + 0.1 * jax.random.normal(splits[15], (D,), jnp.float32), 0.5, 1.5),
        "second_shift": bell_draw(splits[16], (D,), 0.3, 2.0, (), jnp.float32),
        "cotangent": bell_draw(splits[17], (TOKENS, D), 1.0, 6.0, ((0, 32),)),
    }


@jax.custom_vjp
def low(v):
    return lax.optimization_barrier(v.astype(jnp.bfloat16)).astype(jnp.float32)

@jax.custom_vjp
def low_back(v):
    return v

def low_keep(v):
    return (low(v), None)

def low_pass(kept, grad):
    return (grad,)

def back_keep(v):
    return (v, None)

def back_low(kept, grad):
    return (low(grad),)
low.defvjp(low_keep, low_pass)
low_back.defvjp(back_keep, back_low)
highest = lax.Precision.HIGHEST
epsilon = 1e-06
masked_value = -1e+30

def layer_norm(inputs, norm_gain, norm_shift):
    average = lax.optimization_barrier(jnp.mean(inputs, axis=-1, keepdims=True))
    centred = inputs - average
    spread = lax.optimization_barrier(jnp.mean(centred * centred, axis=-1, keepdims=True))
    return centred * lax.rsqrt(spread + epsilon) * norm_gain + norm_shift

def slot_segments(classes, slot_ids):
    counts = (TABLE + (LONG - TABLE) * classes).astype(jnp.int32)
    image_ends = jnp.cumsum(counts).astype(jnp.int32)
    segment = lax.optimization_barrier(jnp.sum((slot_ids[:, None] >= image_ends[None, :]).astype(jnp.int32), axis=1)).astype(jnp.int32)
    return (segment, (image_ends - counts).astype(jnp.int32))

def table_mixing(classes, slot_ids, source_index):
    segment, starts = slot_segments(classes, slot_ids)
    images = jnp.arange(IMG_GRP, dtype=jnp.int32)
    picked = segment[:, None] == images[None, :]
    valid = segment < IMG_GRP
    start_of = lax.optimization_barrier(jnp.sum(jnp.where(picked, starts[None, :], 0), axis=1)).astype(jnp.int32)
    larger = lax.optimization_barrier(jnp.sum(jnp.where(picked, classes[None, :], 0), axis=1)) > 0
    place = jnp.where(valid, slot_ids - start_of, 0).astype(jnp.int32)
    columns = jnp.arange(TABLE, dtype=jnp.int32)
    direct = (place[:, None] == columns[None, :]).astype(jnp.float32)
    positions = jnp.arange(LONG, dtype=jnp.int32)
    sources = lax.optimization_barrier(jnp.sum(jnp.where(place[:, None, None] == positions[None, :, None], source_index[None, :, :], 0), axis=1)).astype(jnp.int32)
    across = ((place * 7 % 12).astype(jnp.float32) + 0.5) / 12.0
    downward = ((place * 5 % 12).astype(jnp.float32) + 0.5) / 12.0
    corners = jnp.stack([(1.0 - across) * (1.0 - downward), (1.0 - across) * downward, across * (1.0 - downward), across * downward], axis=1)
    blended = lax.optimization_barrier(jnp.sum(jnp.where(sources[:, :, None] == columns[None, None, :], corners[:, :, None], 0.0), axis=1))
    mixing = jnp.where((valid & larger)[:, None], blended, jnp.where((valid & ~larger)[:, None], direct, 0.0))
    return (segment, valid, mixing)

def group_forward(grp_tokens, grp_classes, source_index, params):
    position_table, input_weight, query_bias, value_bias, output_weight, output_bias, up_weight, up_bias, down_weight, down_bias, first_gain, first_shift, second_gain, second_shift = params
    slot_ids = jnp.arange(GRP_SLOTS, dtype=jnp.int32)
    segment, valid, mixing = table_mixing(grp_classes, slot_ids, source_index)
    same_image = segment[:, None] == segment[None, :]
    embedded = grp_tokens + jnp.dot(mixing, position_table, precision=highest)
    normed = low(layer_norm(embedded, first_gain, first_shift))
    projected = jnp.dot(normed, input_weight, precision=highest)
    queries = low_back(low(projected[:, :D] + query_bias)).reshape(GRP_SLOTS, HEADS, HEAD_DIM)
    keys_all = low_back(low(projected[:, D:2 * D])).reshape(GRP_SLOTS, HEADS, HEAD_DIM)
    values = low_back(low(projected[:, 2 * D:] + value_bias)).reshape(GRP_SLOTS, HEADS, HEAD_DIM)
    raw_scores = low_back(jnp.einsum('qhd,khd->hqk', queries, keys_all, precision=highest))
    logits = jnp.where(same_image[None], raw_scores * HEAD_DIM ** (-0.5), masked_value)
    row_max = lax.optimization_barrier(jnp.max(logits, axis=-1, keepdims=True))
    log_total = row_max + jnp.log(lax.optimization_barrier(jnp.sum(jnp.exp(logits - row_max), axis=-1, keepdims=True)))
    probs_low = low(jnp.exp(logits - log_total))
    attended = jnp.einsum('hqk,khd->qhd', probs_low, values, precision=highest).reshape(GRP_SLOTS, D)
    attended = low_back(low(attended))
    branch_one = low_back(jnp.dot(attended, output_weight, precision=highest) + output_bias)
    hidden = embedded + branch_one
    second = low(layer_norm(hidden, second_gain, second_shift))
    upper = low_back(jnp.dot(second, up_weight, precision=highest) + up_bias)
    active = low(jax.nn.gelu(upper, approximate=False))
    branch_two = low_back(jnp.dot(active, down_weight, precision=highest) + down_bias)
    return jnp.where(valid[:, None], hidden + branch_two, 0.0)

def reference(tokens, classes, source_index, position_table, input_weight, query_bias, value_bias, output_weight, output_bias, up_weight, up_bias, down_weight, down_bias, first_gain, first_shift, second_gain, second_shift, cotangent):
    params = tuple((member.astype(jnp.float32) for member in (position_table, input_weight, query_bias, value_bias, output_weight, output_bias, up_weight, up_bias, down_weight, down_bias, first_gain, first_shift, second_gain, second_shift)))
    tokens32 = tokens.astype(jnp.float32).reshape(N_IMG, GRP_SLOTS, D)
    grouped_classes = classes.reshape(N_IMG, IMG_GRP)

    def whole_forward(token_input, param_input):

        def one_group(carry, inputs):
            grp_tokens, grp_classes = inputs
            return (carry, group_forward(grp_tokens, grp_classes, source_index, param_input))
        _, outputs = lax.scan(jax.checkpoint(one_group), jnp.zeros((), jnp.float32), (token_input, grouped_classes))
        return outputs
    primal, pullback = jax.vjp(whole_forward, tokens32, params)
    token_grad, param_grads = pullback(cotangent.astype(jnp.float32).reshape(N_IMG, GRP_SLOTS, D))
    return (primal.reshape(TOKENS, D).astype(jnp.bfloat16), token_grad.reshape(TOKENS, D).astype(jnp.bfloat16), param_grads[0], param_grads[1], param_grads[2], param_grads[3], param_grads[4], param_grads[5], param_grads[6], param_grads[7], param_grads[8], param_grads[9], param_grads[10], param_grads[11], param_grads[12], param_grads[13])
```

```python
import jax
import jax.numpy as jnp
from jax import lax
from jax.experimental import pallas as pl
from jax.experimental.pallas import tpu as pltpu
from jax.sharding import PartitionSpec as P

HEADS = 16
HEAD_DIM = 64
TABLE = 50
LONG = 145
IMG_GRP = 4


highest = lax.Precision.HIGHEST
epsilon = 1e-06
masked_value = -1e30


def layer_norm(inputs, norm_gain, norm_shift):
    average = jnp.mean(inputs, axis=-1, keepdims=True)
    centred = inputs - average
    spread = jnp.mean(centred * centred, axis=-1, keepdims=True)
    return centred * lax.rsqrt(spread + epsilon) * norm_gain + norm_shift


def exact_gelu(inputs):
    return jax.nn.gelu(inputs, approximate=False)


def slot_segments(classes, slot_ids):
    counts = TABLE + (LONG - TABLE) * classes
    image_ends = jnp.cumsum(counts)
    segment = jnp.sum((slot_ids[:, None] >= image_ends[None, :]).astype(jnp.int32), axis=1)
    return (segment, image_ends - counts)


def table_mixing(classes, slot_ids, source_index):
    segment, starts = slot_segments(classes, slot_ids)
    images = jnp.arange(IMG_GRP, dtype=jnp.int32)
    picked = segment[:, None] == images[None, :]
    valid = segment < IMG_GRP
    start_of = jnp.sum(jnp.where(picked, starts[None, :], 0), axis=1)
    larger = jnp.sum(jnp.where(picked, classes[None, :], 0), axis=1) > 0
    place = jnp.where(valid, slot_ids - start_of, 0)
    columns = jnp.arange(TABLE, dtype=jnp.int32)
    direct = (place[:, None] == columns[None, :]).astype(jnp.float32)
    positions = jnp.arange(LONG, dtype=jnp.int32)
    sources = jnp.sum(
        jnp.where(place[:, None, None] == positions[None, :, None], source_index[None, :, :], 0),
        axis=1,
    )
    across = ((place * 7 % 12).astype(jnp.float32) + 0.5) / 12.0
    downward = ((place * 5 % 12).astype(jnp.float32) + 0.5) / 12.0
    corners = jnp.stack(
        [
            (1.0 - across) * (1.0 - downward),
            (1.0 - across) * downward,
            across * (1.0 - downward),
            across * downward,
        ],
        axis=1,
    )
    blended = jnp.sum(
        jnp.where(sources[:, :, None] == columns[None, None, :], corners[:, :, None], 0.0), axis=1
    )
    mixing = jnp.where(
        (valid & larger)[:, None], blended, jnp.where((valid & ~larger)[:, None], direct, 0.0)
    )
    return (segment, valid, mixing)


GROUP = 4
f32 = jnp.float32
bf16 = jnp.bfloat16


def exchange(value, axis, distance):
    size = lax.axis_size(axis)
    return lax.ppermute(value, axis, [(i, i ^ distance) for i in range(size)])


def phases(size):
    found, stride = [], size
    while stride > 1:
        radix = 4 if stride % 4 == 0 else 2
        stride //= radix
        found.append((stride, radix))
    return found


def gather_relative(shard):
    parts = {0: shard}
    for stride, radix in phases(lax.axis_size("img")):
        held = dict(parts)
        if len(held) <= 4:
            for j, part in held.items():
                for digit in range(1, radix):
                    parts[j ^ (digit * stride)] = exchange(part, "img", digit * stride)
        else:
            order = sorted(held)
            stacked = jnp.stack([held[j] for j in order])
            for digit in range(1, radix):
                received = exchange(stacked, "img", digit * stride)
                for position, j in enumerate(order):
                    parts[j ^ (digit * stride)] = received[position]
    return [parts[j] for j in range(len(parts))]


def scatter_relative(pieces):
    held = {j: piece for j, piece in enumerate(pieces)}
    for stride, radix in reversed(phases(lax.axis_size("img"))):
        keep = sorted(j for j in held if (j // stride) % radix == 0)
        total = {j: held[j] for j in keep}
        order = [j for j in keep if j != 0] + [0]
        if len(keep) <= 4:
            for j in order:
                for digit in range(1, radix):
                    sent = held[j + digit * stride].astype(bf16)
                    total[j] = total[j] + exchange(sent, "img", digit * stride).astype(f32)
        else:
            for digit in range(1, radix):
                sent = jnp.stack([held[j + digit * stride].astype(bf16) for j in keep])
                received = exchange(sent, "img", digit * stride)
                for position, j in enumerate(keep):
                    total[j] = total[j] + received[position].astype(f32)
        held = total
    return held[0]


def group_gather(value):
    across = exchange(value, "seq", 2)
    return [value, exchange(value, "seq", 1), across, exchange(across, "seq", 1)]


def group_scatter(parts):
    beside = exchange(jnp.stack([parts[3], parts[1]]).astype(bf16), "seq", 1)
    far = parts[2] + beside[0].astype(f32)
    near = parts[0] + beside[1].astype(f32)
    return near + exchange(far.astype(bf16), "seq", 2).astype(f32)


def place_kernel(count):
    def kernel(index_ref, *refs):
        for j in range(count):
            refs[count][index_ref[j]] = refs[j][...]

    return kernel


def place(parts, mine):
    count = len(parts)
    index = mine ^ jnp.arange(count, dtype=jnp.int32)
    return pl.pallas_call(
        place_kernel(count),
        out_shape=jax.ShapeDtypeStruct((count,) + parts[0].shape, parts[0].dtype),
        in_specs=[pl.BlockSpec(memory_space=pltpu.SMEM)]
        + [pl.BlockSpec(memory_space=pltpu.VMEM)] * count,
        out_specs=pl.BlockSpec(memory_space=pltpu.VMEM),
        name="place",
    )(index, *parts)


def sum_everywhere(value):
    rows = value.shape[0] // 2
    seq = lax.axis_index("seq")
    low, high = seq & 1, (seq >> 1) & 1
    halves = value.reshape(2, rows, -1)
    mine = mine_of(halves, low, 0) + exchange(mine_of(halves, 1 - low, 0), "seq", 1)
    halves = mine.reshape(2, rows // 2, -1)
    mine = mine_of(halves, high, 0) + exchange(mine_of(halves, 1 - high, 0), "seq", 2)
    for stride, radix in reversed(phases(lax.axis_size("img"))):
        others = [mine] + [exchange(mine, "img", digit * stride) for digit in range(1, radix)]
        while len(others) > 1:
            others = [others[i] + others[i + 1] for i in range(0, len(others), 2)]
        mine = others[0]
    other = exchange(mine, "seq", 2)
    mine = jnp.where(high == 0, jnp.concatenate([mine, other]), jnp.concatenate([other, mine]))
    other = exchange(mine, "seq", 1)
    return jnp.where(low == 0, jnp.concatenate([mine, other]), jnp.concatenate([other, mine]))


def reorder(parts, mine):
    stacked = jnp.stack(parts)
    return [lax.dynamic_index_in_dim(stacked, mine ^ p, 0, keepdims=False) for p in range(GROUP)]


def mine_of(array, mine, axis):
    return lax.dynamic_index_in_dim(array, mine, axis, keepdims=False)


def on_device(
    tokens,
    classes,
    source_index,
    position_table,
    input_weight,
    query_bias,
    value_bias,
    output_weight,
    output_bias,
    up_weight,
    up_bias,
    down_weight,
    down_bias,
    first_gain,
    first_shift,
    second_gain,
    second_shift,
    cotangent,
):
    shard_rows, width = tokens.shape
    group_slots = shard_rows * GROUP
    size = lax.axis_size("img")
    img, seq = lax.axis_index("img"), lax.axis_index("seq")
    held = width // size
    part = width // GROUP
    heads = HEADS // GROUP
    hidden_units = up_weight.shape[1]
    units = hidden_units // size // GROUP
    scale = HEAD_DIM ** (-0.5)

    input_part = mine_of(input_weight.reshape(held, 3, GROUP, part), seq, 2).reshape(held, 3 * part)
    output_part = mine_of(output_weight.reshape(held, GROUP, part), seq, 1)
    up_part = mine_of(up_weight.reshape(held, size, GROUP, units), seq, 2).reshape(held, size * units)
    down_part = mine_of(down_weight.reshape(GROUP, units, width), seq, 0)
    input_full = place(gather_relative(input_part), img).reshape(width, 3 * part)
    output_cols = place(gather_relative(output_part), img).reshape(GROUP, part, part)
    up_full = place(gather_relative(up_part), img).reshape(width, size * units)
    down_full = place(gather_relative(down_part), img).reshape(size * units, width)
    output_blocks = [mine_of(output_cols, seq, 0)] + [
        exchange(mine_of(output_cols, seq ^ j, 0), "seq", j) for j in range(1, GROUP)
    ]
    output_full = jnp.concatenate(reorder(output_blocks, seq), axis=1)
    query_bias_part = mine_of(query_bias.reshape(GROUP, part), seq, 0)
    value_bias_part = mine_of(value_bias.reshape(GROUP, part), seq, 0)
    up_bias_part = mine_of(up_bias.reshape(size, GROUP, units), seq, 1).reshape(size * units)

    my_slots = seq * shard_rows + jnp.arange(shard_rows, dtype=jnp.int32)
    _, valid, mixing = table_mixing(classes, my_slots, source_index)
    owners = seq ^ jnp.arange(GROUP, dtype=jnp.int32)
    all_slots = (owners[:, None] * shard_rows + jnp.arange(shard_rows, dtype=jnp.int32)[None]).reshape(-1)
    all_segments, _ = slot_segments(classes, all_slots)
    same_image = all_segments[:, None] == all_segments[None, :]

    upstream = jnp.where(valid[:, None], cotangent.astype(f32), 0.0)
    upstream_all = jnp.concatenate(group_gather(upstream.astype(bf16)), axis=0)

    embedded = tokens.astype(f32) + jnp.dot(mixing, position_table, precision=highest)
    first_value, first_pull = jax.vjp(layer_norm, embedded, first_gain, first_shift)
    normed_all = jnp.concatenate(group_gather(first_value.astype(bf16)), axis=0)
    projected = jnp.dot(normed_all, input_full, preferred_element_type=f32)

    def split_heads(value):
        return value.astype(bf16).reshape(group_slots, heads, HEAD_DIM)

    queries = split_heads(projected[:, :part] + query_bias_part)
    keys = split_heads(projected[:, part : 2 * part])
    values = split_heads(projected[:, 2 * part :] + value_bias_part)
    raw_scores = jnp.einsum("qhd,khd->hqk", queries, keys, preferred_element_type=f32)
    logits = jnp.where(same_image[None], raw_scores * scale, masked_value)
    row_max = jnp.max(logits, axis=-1, keepdims=True)
    log_total = row_max + jnp.log(jnp.sum(jnp.exp(logits - row_max), axis=-1, keepdims=True))
    probs = jnp.exp(logits - log_total)
    probs_low = probs.astype(bf16)
    attended = (
        jnp.einsum("hqk,khd->qhd", probs_low, values, preferred_element_type=f32)
        .reshape(group_slots, part)
        .astype(bf16)
    )

    def row_parts(value):
        return [value[j * shard_rows : (j + 1) * shard_rows] for j in range(GROUP)]

    branch_one = group_scatter(row_parts(jnp.dot(attended, output_full, preferred_element_type=f32)))
    hidden = embedded + branch_one + output_bias
    second_value, second_pull = jax.vjp(layer_norm, hidden, second_gain, second_shift)
    second_all = jnp.concatenate(group_gather(second_value.astype(bf16)), axis=0)
    upper = jnp.dot(second_all, up_full, preferred_element_type=f32) + up_bias_part
    active, gelu_pull = jax.vjp(exact_gelu, upper)
    active_low = active.astype(bf16)

    def to_owners(term, rows):
        pieces = term.reshape(size, rows, term.shape[1])
        return scatter_relative([mine_of(pieces, img ^ j, 0) for j in range(size)])

    def columns_of_all(total):
        return reorder(group_gather(total.astype(bf16)), seq)

    down_sum = to_owners(
        jnp.einsum("sf,sd->fd", active_low, upstream_all, preferred_element_type=f32), units
    )
    active_grad = jnp.einsum("sd,fd->sf", upstream_all, down_full, preferred_element_type=f32)
    upper_low = gelu_pull(active_grad)[0].astype(bf16)
    second_grad = group_scatter(
        row_parts(jnp.einsum("sf,df->sd", upper_low, up_full, preferred_element_type=f32))
    )
    up_sum = to_owners(
        jnp.einsum("sd,sf->df", second_all, upper_low, preferred_element_type=f32), held
    )
    branch_two = group_scatter(row_parts(jnp.dot(active_low, down_full, preferred_element_type=f32)))
    block_out = jnp.where(valid[:, None], hidden + branch_two + down_bias, 0.0).astype(bf16)

    hidden_grad, second_gain_grad, second_shift_grad = second_pull(second_grad)
    hidden_grad = hidden_grad + upstream
    branch_low = hidden_grad.astype(bf16)
    branch_all = jnp.concatenate(group_gather(branch_low), axis=0)
    output_term = jnp.einsum("sc,sd->cd", attended, branch_all, preferred_element_type=f32)
    output_term = output_term.astype(bf16).reshape(part, GROUP, part)
    term_blocks = [mine_of(output_term, seq, 1)] + [
        exchange(mine_of(output_term, seq ^ j, 1), "seq", j) for j in range(1, GROUP)
    ]
    output_sum = to_owners(jnp.concatenate(reorder(term_blocks, seq), axis=0).astype(f32), held)

    attended_grad = jnp.einsum(
        "sd,cd->sc", branch_all, output_full, preferred_element_type=f32
    )
    attended_grad = split_heads(attended_grad)
    probs_grad = jnp.einsum("qhd,khd->hqk", attended_grad, values, preferred_element_type=f32)
    inner = jnp.sum(probs * probs_grad, axis=-1, keepdims=True)
    score_low = (scale * (probs * (probs_grad - inner))).astype(bf16)
    query_grad = jnp.einsum("hqk,khd->qhd", score_low, keys, preferred_element_type=f32)
    key_grad = jnp.einsum("hqk,qhd->khd", score_low, queries, preferred_element_type=f32)
    value_grad = jnp.einsum("hqk,qhd->khd", probs_low, attended_grad, preferred_element_type=f32)
    projection_grad = jnp.concatenate(
        [grad.reshape(group_slots, part).astype(bf16) for grad in (query_grad, key_grad, value_grad)],
        axis=1,
    )
    input_sum = to_owners(
        jnp.einsum("sd,se->de", normed_all, projection_grad, preferred_element_type=f32), held
    )
    normed_grad = group_scatter(
        row_parts(jnp.einsum("se,de->sd", projection_grad, input_full, preferred_element_type=f32))
    )
    embedded_grad, first_gain_grad, first_shift_grad = first_pull(normed_grad)
    embedded_grad = embedded_grad + hidden_grad
    table_term = jnp.einsum("st,sd->td", mixing, embedded_grad, precision=highest)

    input_columns = [c.reshape(held, 3, part) for c in columns_of_all(input_sum)]
    input_weight_grad = jnp.stack(input_columns, axis=2).reshape(held, 3 * width).astype(f32)
    output_weight_grad = jnp.concatenate(columns_of_all(output_sum), axis=1).astype(f32)
    up_columns = [c.reshape(held, size, units) for c in columns_of_all(up_sum)]
    up_weight_grad = jnp.stack(up_columns, axis=2).reshape(held, hidden_units).astype(f32)
    down_weight_grad = jnp.concatenate(columns_of_all(down_sum), axis=0).astype(f32)

    def spread(value, shape, axis):
        value = jnp.expand_dims(value.reshape(shape), axis)
        mask = jnp.arange(GROUP, dtype=jnp.int32).reshape([-1 if a == axis else 1 for a in range(value.ndim)])
        return jnp.where(mask == seq, value, 0.0).reshape(-1)

    def columns(value):
        return jnp.sum(value.astype(f32), axis=0)

    projection_sums = columns(projection_grad)
    rows = [
        table_term,
        spread(projection_sums[:part], (part,), 0),
        spread(projection_sums[2 * part :], (part,), 0),
        columns(branch_low),
        columns(upstream),
        first_gain_grad,
        first_shift_grad,
        second_gain_grad,
        second_shift_grad,
        spread(columns(upper_low), (size, units), 1),
    ]
    packed = jnp.concatenate([row.reshape(-1, width) for row in rows])
    used = packed.shape[0]
    packed = jnp.pad(packed, ((0, -used % 32), (0, 0)))
    total = sum_everywhere(packed)
    vectors = total[TABLE:used]
    return (
        block_out,
        embedded_grad.astype(bf16),
        total[:TABLE],
        input_weight_grad,
        vectors[0],
        vectors[1],
        output_weight_grad,
        vectors[2],
        up_weight_grad,
        vectors[8:].reshape(-1),
        down_weight_grad,
        vectors[3],
        vectors[4],
        vectors[5],
        vectors[6],
        vectors[7],
    )


def solution(mesh):
    placed = (
        P(("img", "seq"), None),
        P("img"),
        P(),
        P(),
        P("img", None),
        P(),
        P(),
        P("img", None),
        P(),
        P("img", None),
        P(),
        P("img", None),
        P(),
        P(),
        P(),
        P(),
        P(),
        P(("img", "seq"), None),
    )
    return jax.shard_map(
        on_device,
        mesh=mesh,
        in_specs=placed,
        out_specs=(
            P(("img", "seq"), None),
            P(("img", "seq"), None),
            P(),
            P("img", None),
            P(),
            P(),
            P("img", None),
            P(),
            P("img", None),
            P(),
            P("img", None),
            P(),
            P(),
            P(),
            P(),
            P(),
        ),
        check_vma=False,
    )
```

```python
import jax
import jax.numpy as jnp
from jax import lax
from jax.experimental import pallas as pl
from jax.experimental.pallas import tpu as pltpu
from jax.sharding import PartitionSpec as P

HEADS = 16
HEAD_DIM = 64
TABLE = 50
LONG = 145
IMG_GRP = 4


highest = lax.Precision.HIGHEST
epsilon = 1e-06
masked_value = -1e30


def layer_norm(inputs, norm_gain, norm_shift):
    average = jnp.mean(inputs, axis=-1, keepdims=True)
    centred = inputs - average
    spread = jnp.mean(centred * centred, axis=-1, keepdims=True)
    return centred * lax.rsqrt(spread + epsilon) * norm_gain + norm_shift


def exact_gelu(inputs):
    return jax.nn.gelu(inputs, approximate=False)


def slot_segments(classes, slot_ids):
    counts = TABLE + (LONG - TABLE) * classes
    image_ends = jnp.cumsum(counts)
    segment = jnp.sum((slot_ids[:, None] >= image_ends[None, :]).astype(jnp.int32), axis=1)
    return (segment, image_ends - counts)


def table_mixing(classes, slot_ids, source_index):
    segment, starts = slot_segments(classes, slot_ids)
    images = jnp.arange(IMG_GRP, dtype=jnp.int32)
    picked = segment[:, None] == images[None, :]
    valid = segment < IMG_GRP
    start_of = jnp.sum(jnp.where(picked, starts[None, :], 0), axis=1)
    larger = jnp.sum(jnp.where(picked, classes[None, :], 0), axis=1) > 0
    place = jnp.where(valid, slot_ids - start_of, 0)
    columns = jnp.arange(TABLE, dtype=jnp.int32)
    direct = (place[:, None] == columns[None, :]).astype(jnp.float32)
    positions = jnp.arange(LONG, dtype=jnp.int32)
    sources = jnp.sum(
        jnp.where(place[:, None, None] == positions[None, :, None], source_index[None, :, :], 0),
        axis=1,
    )
    across = ((place * 7 % 12).astype(jnp.float32) + 0.5) / 12.0
    downward = ((place * 5 % 12).astype(jnp.float32) + 0.5) / 12.0
    corners = jnp.stack(
        [
            (1.0 - across) * (1.0 - downward),
            (1.0 - across) * downward,
            across * (1.0 - downward),
            across * downward,
        ],
        axis=1,
    )
    blended = jnp.sum(
        jnp.where(sources[:, :, None] == columns[None, None, :], corners[:, :, None], 0.0), axis=1
    )
    mixing = jnp.where(
        (valid & larger)[:, None], blended, jnp.where((valid & ~larger)[:, None], direct, 0.0)
    )
    return (segment, valid, mixing)


GROUP = 4
f32 = jnp.float32
bf16 = jnp.bfloat16


def exchange(value, axis, distance):
    size = lax.axis_size(axis)
    return lax.ppermute(value, axis, [(i, i ^ distance) for i in range(size)])


def phases(size):
    found, stride = [], size
    while stride > 1:
        radix = 4 if stride % 4 == 0 else 2
        stride //= radix
        found.append((stride, radix))
    return found


def gather_relative(shard):
    parts = {0: shard}
    for stride, radix in phases(lax.axis_size("img")):
        held = dict(parts)
        if len(held) <= 4:
            for j, part in held.items():
                for digit in range(1, radix):
                    parts[j ^ (digit * stride)] = exchange(part, "img", digit * stride)
        else:
            order = sorted(held)
            stacked = jnp.stack([held[j] for j in order])
            for digit in range(1, radix):
                received = exchange(stacked, "img", digit * stride)
                for position, j in enumerate(order):
                    parts[j ^ (digit * stride)] = received[position]
    return [parts[j] for j in range(len(parts))]


def scatter_relative(pieces):
    held = {j: piece for j, piece in enumerate(pieces)}
    for stride, radix in reversed(phases(lax.axis_size("img"))):
        keep = sorted(j for j in held if (j // stride) % radix == 0)
        total = {j: held[j] for j in keep}
        order = [j for j in keep if j != 0] + [0]
        if len(keep) <= 4:
            for j in order:
                for digit in range(1, radix):
                    sent = held[j + digit * stride].astype(bf16)
                    total[j] = total[j] + exchange(sent, "img", digit * stride).astype(f32)
        else:
            for digit in range(1, radix):
                sent = jnp.stack([held[j + digit * stride].astype(bf16) for j in keep])
                received = exchange(sent, "img", digit * stride)
                for position, j in enumerate(keep):
                    total[j] = total[j] + received[position].astype(f32)
        held = total
    return held[0]


def group_gather(value):
    across = exchange(value, "seq", 2)
    beside = exchange(value, "seq", 1)
    return [value, beside, across, exchange(across, "seq", 1)]


def group_scatter(parts):
    beside = exchange(jnp.stack([parts[3], parts[1]]).astype(bf16), "seq", 1)
    far = parts[2] + beside[0].astype(f32)
    near = parts[0] + beside[1].astype(f32)
    return near + exchange(far.astype(bf16), "seq", 2).astype(f32)


def place_kernel(count):
    def kernel(index_ref, *refs):
        for j in range(count):
            refs[count][index_ref[j]] = refs[j][...]

    return kernel


def place(parts, mine):
    count = len(parts)
    index = mine ^ jnp.arange(count, dtype=jnp.int32)
    return pl.pallas_call(
        place_kernel(count),
        out_shape=jax.ShapeDtypeStruct((count,) + parts[0].shape, parts[0].dtype),
        in_specs=[pl.BlockSpec(memory_space=pltpu.SMEM)]
        + [pl.BlockSpec(memory_space=pltpu.VMEM)] * count,
        out_specs=pl.BlockSpec(memory_space=pltpu.VMEM),
        name="place",
    )(index, *parts)


def sum_everywhere(value):
    rows = value.shape[0] // 2
    seq = lax.axis_index("seq")
    low, high = seq & 1, (seq >> 1) & 1
    halves = value.reshape(2, rows, -1)
    mine = mine_of(halves, low, 0) + exchange(mine_of(halves, 1 - low, 0), "seq", 1)
    halves = mine.reshape(2, rows // 2, -1)
    mine = mine_of(halves, high, 0) + exchange(mine_of(halves, 1 - high, 0), "seq", 2)
    for stride, radix in reversed(phases(lax.axis_size("img"))):
        others = [mine] + [exchange(mine, "img", digit * stride) for digit in range(1, radix)]
        while len(others) > 1:
            others = [others[i] + others[i + 1] for i in range(0, len(others), 2)]
        mine = others[0]
    other = exchange(mine, "seq", 2)
    mine = jnp.where(high == 0, jnp.concatenate([mine, other]), jnp.concatenate([other, mine]))
    other = exchange(mine, "seq", 1)
    return jnp.where(low == 0, jnp.concatenate([mine, other]), jnp.concatenate([other, mine]))


def reorder(parts, mine):
    stacked = jnp.stack(parts)
    return [lax.dynamic_index_in_dim(stacked, mine ^ p, 0, keepdims=False) for p in range(GROUP)]


def mine_of(array, mine, axis):
    return lax.dynamic_index_in_dim(array, mine, axis, keepdims=False)


VMEM = pl.BlockSpec(memory_space=pltpu.VMEM)
SMEM = pl.BlockSpec(memory_space=pltpu.SMEM)
ROWS = (((0,), (0,)), ((), ()))
LAST = (((1,), (1,)), ((), ()))


def local_call(kernel, outs, inputs, scratch=()):
    return pl.pallas_call(
        kernel,
        out_shape=[jax.ShapeDtypeStruct(shape, kind) for shape, kind in outs],
        in_specs=[SMEM] + [VMEM] * (len(inputs) - 1),
        out_specs=[VMEM] * len(outs),
        scratch_shapes=list(scratch),
        compiler_params=pltpu.CompilerParams(vmem_limit_bytes=56 * 1024 * 1024),
    )(*inputs)


def pick(sources, blocks, outs, index):
    count = len(blocks)

    def kernel(index_ref, *refs):
        ins, results, sems = refs[: len(sources)], refs[len(sources) : -1], refs[-1]
        copies = []
        for number, (source, axis, start, out, there, length) in enumerate(blocks):
            begin = pl.multiple_of(start + index_ref[0] * length, length)
            if axis == 0:
                origin, target = ins[source].at[pl.ds(begin, length), :], results[out]
            else:
                origin = ins[source].at[:, pl.ds(begin, length)]
                target = results[out].at[:, pl.ds(there, length)]
            copies.append(pltpu.make_async_copy(origin, target, sems.at[number]))
        for copy in copies:
            copy.start()
        for copy in copies:
            copy.wait()

    return pl.pallas_call(
        kernel,
        out_shape=[jax.ShapeDtypeStruct(shape, bf16) for shape in outs],
        in_specs=[SMEM] + [pl.BlockSpec(memory_space=pl.ANY)] * len(sources),
        out_specs=[VMEM] * len(outs),
        scratch_shapes=[pltpu.SemaphoreType.DMA((count,))],
    )(index, *sources)


def place_in(index_ref, parts, out, source, target):
    rows = parts[0].shape[0]
    for j, part in enumerate(parts):
        at = pl.ds(pl.multiple_of(index_ref[j] * rows, rows), rows)
        out[at, target[0] : target[1]] = part[:, source[0] : source[1]]


def attention_forward(index, normed, firsts, seconds, query_bias, value_bias, segments):
    slots, width = normed.shape
    part = width // GROUP
    heads = part // HEAD_DIM
    rows = slots // GROUP
    count = len(firsts)
    scale = HEAD_DIM ** (-0.5)

    def kernel(index_ref, x_ref, *refs):
        halves, refs = (refs[:count], refs[count : 2 * count]), refs[2 * count :]
        qb_ref, vb_ref, seg_rows, seg_cols = refs[:4]
        w_out, wo_out, q_out, k_out, v_out, att_out, total_out = refs[4:]
        place_in(index_ref, halves[0], w_out, (0, 2 * part), (0, 2 * part))
        place_in(index_ref, halves[1], w_out, (0, part), (2 * part, 3 * part))
        place_in(index_ref, halves[1], wo_out, (part, 2 * part), (0, part))
        projected = jnp.dot(x_ref[...], w_out[...], preferred_element_type=f32)
        queries = (projected[:, :part] + qb_ref[...]).astype(bf16)
        for block in range(GROUP):
            q_out[block] = queries[block * rows : (block + 1) * rows]
        k_out[...] = projected[:, part : 2 * part].astype(bf16)
        v_out[...] = (projected[:, 2 * part :] + vb_ref[...]).astype(bf16)

        def step(block, carry):
            same = seg_rows[block] == seg_cols[...]
            mixed, totals = [], []
            for h in range(heads):
                lanes = slice(h * HEAD_DIM, (h + 1) * HEAD_DIM)
                raw = lax.dot_general(
                    q_out[block, :, lanes], k_out[:, lanes], LAST, preferred_element_type=f32
                )
                logits = jnp.where(same, raw * scale, masked_value)
                top = jnp.max(logits, axis=-1, keepdims=True)
                raised = jnp.exp(logits - top)
                total = jnp.sum(raised, axis=-1, keepdims=True)
                probs = (raised * (1.0 / total)).astype(bf16)
                mixed.append(jnp.dot(probs, v_out[:, lanes], preferred_element_type=f32))
                totals.append(top + jnp.log(total))
            att_out[block] = jnp.concatenate(mixed, axis=1).astype(bf16)
            total_out[block] = jnp.concatenate(totals, axis=1)
            return carry

        lax.fori_loop(0, GROUP, step, 0)

    outs = [
        ((width, 3 * part), bf16),
        ((width, part), bf16),
        ((GROUP, rows, part), bf16),
        ((slots, part), bf16),
        ((slots, part), bf16),
        ((GROUP, rows, part), bf16),
        ((GROUP, rows, heads), f32),
    ]
    inputs = [index, normed, *firsts, *seconds, query_bias[None], value_bias[None]]
    inputs += [segments.reshape(GROUP, rows, 1), segments[None]]
    return local_call(kernel, outs, inputs)


def attention_backward(queries, keys, values, mixed_grad, totals, segments):
    blocks, rows, part = queries.shape
    slots = keys.shape[0]
    heads = part // HEAD_DIM
    scale = HEAD_DIM ** (-0.5)

    def kernel(zero_ref, q_ref, k_ref, v_ref, g_ref, t_ref, seg_rows, seg_cols, out, sums, acc):
        acc[...] = jnp.zeros_like(acc)

        def step(block, carry):
            same = seg_rows[block] == seg_cols[...]
            q_grads, k_grads, v_grads = [], [], []
            for h in range(heads):
                lanes = slice(h * HEAD_DIM, (h + 1) * HEAD_DIM)
                query, key, grad = q_ref[block, :, lanes], k_ref[:, lanes], g_ref[block, :, lanes]
                raw = lax.dot_general(query, key, LAST, preferred_element_type=f32)
                logits = jnp.where(same, raw * scale, masked_value)
                probs = jnp.exp(logits - t_ref[block, :, h : h + 1])
                probs_grad = lax.dot_general(
                    grad, v_ref[:, lanes], LAST, preferred_element_type=f32
                )
                weighted = probs * probs_grad
                inner = jnp.sum(weighted, axis=-1, keepdims=True)
                score = (scale * (weighted - probs * inner)).astype(bf16)
                q_grads.append(jnp.dot(score, key, preferred_element_type=f32))
                k_grads.append(
                    lax.dot_general(score, query, ROWS, preferred_element_type=f32)
                )
                v_grads.append(
                    lax.dot_general(probs.astype(bf16), grad, ROWS, preferred_element_type=f32)
                )
            start = pl.multiple_of(block * rows, 8)
            acc[pl.ds(start, rows), :part] = jnp.concatenate(q_grads, axis=1)
            acc[:, part:] += jnp.concatenate(k_grads + v_grads, axis=1)
            return carry

        lax.fori_loop(0, blocks, step, 0)
        rounded = acc[...].astype(bf16)
        out[...] = rounded
        sums[...] = jnp.sum(rounded.astype(f32), axis=0, keepdims=True)

    outs = [((slots, 3 * part), bf16), ((1, 3 * part), f32)]
    inputs = [jnp.zeros((1,), jnp.int32), queries, keys, values]
    inputs += [mixed_grad.reshape(blocks, rows, part), totals]
    inputs += [segments.reshape(blocks, rows, 1), segments[None]]
    scratch = [pltpu.VMEM((slots, 3 * part), f32)]
    return local_call(kernel, outs, inputs, scratch)


def feed_forward(index, seconds, parts, bias):
    rows, width = seconds[0].shape
    count, units = len(parts), parts[0].shape[1]
    half = 0.5**0.5

    def kernel(index_ref, *refs):
        xs, refs = refs[:GROUP], refs[GROUP:]
        weights, refs = refs[:count], refs[count:]
        b_ref, w_out, x_out, active_out, slope_out, upper = refs
        place_in(index_ref, weights, w_out, (0, units), (0, units))
        for j in range(GROUP):
            x_out[j] = xs[j][...]
            upper[...] = jnp.dot(xs[j][...], w_out[...], preferred_element_type=f32) + b_ref[...]

            def step(i, carry, j=j):
                at = pl.ds(pl.multiple_of(i * 8, 8), 8)
                u = upper[at, :]
                share = 0.5 * (1.0 + lax.erf(u * half))
                upper[at, :] = u * share
                slope_out[j, at, :] = share + u * jnp.exp(-0.5 * u * u) * 0.3989422804014327
                return carry

            lax.fori_loop(0, rows // 8, step, 0)
            active_out[j] = upper[...].astype(bf16)

    outs = [
        ((width, units), bf16),
        ((GROUP, rows, width), bf16),
        ((GROUP, rows, units), bf16),
        ((GROUP, rows, units), f32),
    ]
    inputs = [index, *seconds, *parts, bias[None]]
    return local_call(kernel, outs, inputs, [pltpu.VMEM((rows, units), f32)])


def feed_backward(index, upstream, parts, slope, up_full):
    blocks, rows, units = slope.shape
    width = upstream.shape[-1]
    count = len(parts)

    def kernel(index_ref, g_ref, *refs):
        weights, refs = refs[:count], refs[count:]
        s_ref, up_ref, w_out, upper_out, sums, sent, kept = refs
        place_in(index_ref, weights, w_out, (0, width), (0, width))
        for j in (3, 1, 2, 0):
            grad = lax.dot_general(g_ref[j], w_out[...], LAST, preferred_element_type=f32)
            low = (grad * s_ref[j]).astype(bf16)
            upper_out[j] = low
            total = jnp.sum(low.astype(f32), axis=0, keepdims=True)
            sums[...] = total if j == 3 else sums[...] + total
            back = lax.dot_general(low, up_ref[...], LAST, preferred_element_type=f32)
            if j % 2:
                sent[(3 - j) // 2] = back.astype(bf16)
            else:
                kept[(2 - j) // 2] = back

    outs = [
        ((count * parts[0].shape[0], width), bf16),
        ((blocks, rows, units), bf16),
        ((1, units), f32),
        ((2, rows, width), bf16),
        ((2, rows, width), f32),
    ]
    return local_call(kernel, outs, [index, upstream, *parts, slope, up_full])


def weight_pieces(index, left, right):
    count = index.shape[0]
    rows = left.shape[1] // count
    shape = (count // 2, rows, right.shape[1])

    def kernel(index_ref, left_ref, right_ref, sent, kept):
        for j in [*range(1, count, 2), *range(0, count, 2)]:
            block = left_ref[:, pl.ds(pl.multiple_of(index_ref[j] * rows, rows), rows)]
            term = lax.dot_general(block, right_ref[...], ROWS, preferred_element_type=f32)
            if j % 2:
                sent[j // 2] = term.astype(bf16)
            else:
                kept[j // 2] = term

    return local_call(kernel, [(shape, bf16), (shape, f32)], [index, left, right])


def group_terms(owners, left, right):
    columns = right.shape[1] // GROUP

    def kernel(owner_ref, left_ref, right_ref, *outs):
        for j in range(GROUP):
            start = pl.multiple_of(owner_ref[j] * columns, columns)
            block = right_ref[:, pl.ds(start, columns)]
            term = lax.dot_general(left_ref[...], block, ROWS, preferred_element_type=f32)
            outs[j][...] = term.astype(bf16)

    shape = ((left.shape[1], columns), bf16)
    return local_call(kernel, [shape] * GROUP, [owners, left, right])


def scatter_pieces(pieces):
    sent, kept = pieces
    total = kept + exchange(sent, "img", 1).astype(f32)
    result = total[0]
    for digit in range(1, total.shape[0]):
        moved = exchange(total[digit].astype(bf16), "img", 2 * digit)
        result = result + moved.astype(f32)
    return result


def spread_columns(owners, parts, repeats):
    rows, total = parts[0].shape
    size = total // repeats

    def kernel(owner_ref, *refs):
        for j in range(GROUP):
            for r in range(repeats):
                start = pl.multiple_of((r * GROUP + owner_ref[j]) * size, size)
                value = refs[j][:, r * size : (r + 1) * size].astype(f32)
                refs[GROUP][:, pl.ds(start, size)] = value

    return local_call(kernel, [((rows, total * GROUP), f32)], [owners, *parts])[0]


def spread_rows(owners, parts):
    rows, columns = parts[0].shape

    def kernel(owner_ref, *refs):
        for j in range(GROUP):
            start = pl.multiple_of(owner_ref[j] * rows, rows)
            refs[GROUP][pl.ds(start, rows), :] = refs[j][...].astype(f32)

    return local_call(kernel, [((rows * GROUP, columns), f32)], [owners, *parts])[0]


def generic_device(
    tokens,
    classes,
    source_index,
    position_table,
    input_weight,
    query_bias,
    value_bias,
    output_weight,
    output_bias,
    up_weight,
    up_bias,
    down_weight,
    down_bias,
    first_gain,
    first_shift,
    second_gain,
    second_shift,
    cotangent,
):
    shard_rows, width = tokens.shape
    group_slots = shard_rows * GROUP
    size = lax.axis_size("img")
    img, seq = lax.axis_index("img"), lax.axis_index("seq")
    held = width // size
    part = width // GROUP
    heads = HEADS // GROUP
    hidden_units = up_weight.shape[1]
    units = hidden_units // size // GROUP
    scale = HEAD_DIM ** (-0.5)

    input_part = mine_of(input_weight.reshape(held, 3, GROUP, part), seq, 2).reshape(held, 3 * part)
    output_part = mine_of(output_weight.reshape(held, GROUP, part), seq, 1)
    up_part = mine_of(up_weight.reshape(held, size, GROUP, units), seq, 2).reshape(held, size * units)
    down_part = mine_of(down_weight.reshape(GROUP, units, width), seq, 0)
    input_full = place(gather_relative(input_part), img).reshape(width, 3 * part)
    output_cols = place(gather_relative(output_part), img).reshape(GROUP, part, part)
    up_full = place(gather_relative(up_part), img).reshape(width, size * units)
    down_full = place(gather_relative(down_part), img).reshape(size * units, width)
    output_blocks = [mine_of(output_cols, seq, 0)] + [
        exchange(mine_of(output_cols, seq ^ j, 0), "seq", j) for j in range(1, GROUP)
    ]
    output_full = jnp.concatenate(reorder(output_blocks, seq), axis=1)
    query_bias_part = mine_of(query_bias.reshape(GROUP, part), seq, 0)
    value_bias_part = mine_of(value_bias.reshape(GROUP, part), seq, 0)
    up_bias_part = mine_of(up_bias.reshape(size, GROUP, units), seq, 1).reshape(size * units)

    my_slots = seq * shard_rows + jnp.arange(shard_rows, dtype=jnp.int32)
    _, valid, mixing = table_mixing(classes, my_slots, source_index)
    owners = seq ^ jnp.arange(GROUP, dtype=jnp.int32)
    all_slots = (owners[:, None] * shard_rows + jnp.arange(shard_rows, dtype=jnp.int32)[None]).reshape(-1)
    all_segments, _ = slot_segments(classes, all_slots)
    same_image = all_segments[:, None] == all_segments[None, :]

    upstream = jnp.where(valid[:, None], cotangent.astype(f32), 0.0)
    upstream_all = jnp.concatenate(group_gather(upstream.astype(bf16)), axis=0)

    embedded = tokens.astype(f32) + jnp.dot(mixing, position_table, precision=highest)
    first_value, first_pull = jax.vjp(layer_norm, embedded, first_gain, first_shift)
    normed_all = jnp.concatenate(group_gather(first_value.astype(bf16)), axis=0)
    projected = jnp.dot(normed_all, input_full, preferred_element_type=f32)

    def split_heads(value):
        return value.astype(bf16).reshape(group_slots, heads, HEAD_DIM)

    queries = split_heads(projected[:, :part] + query_bias_part)
    keys = split_heads(projected[:, part : 2 * part])
    values = split_heads(projected[:, 2 * part :] + value_bias_part)
    raw_scores = jnp.einsum("qhd,khd->hqk", queries, keys, preferred_element_type=f32)
    logits = jnp.where(same_image[None], raw_scores * scale, masked_value)
    row_max = jnp.max(logits, axis=-1, keepdims=True)
    log_total = row_max + jnp.log(jnp.sum(jnp.exp(logits - row_max), axis=-1, keepdims=True))
    probs = jnp.exp(logits - log_total)
    probs_low = probs.astype(bf16)
    attended = (
        jnp.einsum("hqk,khd->qhd", probs_low, values, preferred_element_type=f32)
        .reshape(group_slots, part)
        .astype(bf16)
    )

    def row_parts(value):
        return [value[j * shard_rows : (j + 1) * shard_rows] for j in range(GROUP)]

    branch_one = group_scatter(row_parts(jnp.dot(attended, output_full, preferred_element_type=f32)))
    hidden = embedded + branch_one + output_bias
    second_value, second_pull = jax.vjp(layer_norm, hidden, second_gain, second_shift)
    second_all = jnp.concatenate(group_gather(second_value.astype(bf16)), axis=0)
    upper = jnp.dot(second_all, up_full, preferred_element_type=f32) + up_bias_part
    active, gelu_pull = jax.vjp(exact_gelu, upper)
    active_low = active.astype(bf16)

    def to_owners(term, rows):
        pieces = term.reshape(size, rows, term.shape[1])
        return scatter_relative([mine_of(pieces, img ^ j, 0) for j in range(size)])

    def columns_of_all(total):
        return reorder(group_gather(total.astype(bf16)), seq)

    down_sum = to_owners(
        jnp.einsum("sf,sd->fd", active_low, upstream_all, preferred_element_type=f32), units
    )
    active_grad = jnp.einsum("sd,fd->sf", upstream_all, down_full, preferred_element_type=f32)
    upper_low = gelu_pull(active_grad)[0].astype(bf16)
    second_grad = group_scatter(
        row_parts(jnp.einsum("sf,df->sd", upper_low, up_full, preferred_element_type=f32))
    )
    up_sum = to_owners(
        jnp.einsum("sd,sf->df", second_all, upper_low, preferred_element_type=f32), held
    )
    branch_two = group_scatter(row_parts(jnp.dot(active_low, down_full, preferred_element_type=f32)))
    block_out = jnp.where(valid[:, None], hidden + branch_two + down_bias, 0.0).astype(bf16)

    hidden_grad, second_gain_grad, second_shift_grad = second_pull(second_grad)
    hidden_grad = hidden_grad + upstream
    branch_low = hidden_grad.astype(bf16)
    branch_all = jnp.concatenate(group_gather(branch_low), axis=0)
    output_term = jnp.einsum("sc,sd->cd", attended, branch_all, preferred_element_type=f32)
    output_term = output_term.astype(bf16).reshape(part, GROUP, part)
    term_blocks = [mine_of(output_term, seq, 1)] + [
        exchange(mine_of(output_term, seq ^ j, 1), "seq", j) for j in range(1, GROUP)
    ]
    output_sum = to_owners(jnp.concatenate(reorder(term_blocks, seq), axis=0).astype(f32), held)

    attended_grad = jnp.einsum(
        "sd,cd->sc", branch_all, output_full, preferred_element_type=f32
    )
    attended_grad = split_heads(attended_grad)
    probs_grad = jnp.einsum("qhd,khd->hqk", attended_grad, values, preferred_element_type=f32)
    inner = jnp.sum(probs * probs_grad, axis=-1, keepdims=True)
    score_low = (scale * (probs * (probs_grad - inner))).astype(bf16)
    query_grad = jnp.einsum("hqk,khd->qhd", score_low, keys, preferred_element_type=f32)
    key_grad = jnp.einsum("hqk,qhd->khd", score_low, queries, preferred_element_type=f32)
    value_grad = jnp.einsum("hqk,qhd->khd", probs_low, attended_grad, preferred_element_type=f32)
    projection_grad = jnp.concatenate(
        [grad.reshape(group_slots, part).astype(bf16) for grad in (query_grad, key_grad, value_grad)],
        axis=1,
    )
    input_sum = to_owners(
        jnp.einsum("sd,se->de", normed_all, projection_grad, preferred_element_type=f32), held
    )
    normed_grad = group_scatter(
        row_parts(jnp.einsum("se,de->sd", projection_grad, input_full, preferred_element_type=f32))
    )
    embedded_grad, first_gain_grad, first_shift_grad = first_pull(normed_grad)
    embedded_grad = embedded_grad + hidden_grad
    table_term = jnp.einsum("st,sd->td", mixing, embedded_grad, precision=highest)

    input_columns = [c.reshape(held, 3, part) for c in columns_of_all(input_sum)]
    input_weight_grad = jnp.stack(input_columns, axis=2).reshape(held, 3 * width).astype(f32)
    output_weight_grad = jnp.concatenate(columns_of_all(output_sum), axis=1).astype(f32)
    up_columns = [c.reshape(held, size, units) for c in columns_of_all(up_sum)]
    up_weight_grad = jnp.stack(up_columns, axis=2).reshape(held, hidden_units).astype(f32)
    down_weight_grad = jnp.concatenate(columns_of_all(down_sum), axis=0).astype(f32)

    def spread(value, shape, axis):
        value = jnp.expand_dims(value.reshape(shape), axis)
        mask = jnp.arange(GROUP, dtype=jnp.int32).reshape([-1 if a == axis else 1 for a in range(value.ndim)])
        return jnp.where(mask == seq, value, 0.0).reshape(-1)

    def columns(value):
        return jnp.sum(value.astype(f32), axis=0)

    projection_sums = columns(projection_grad)
    rows = [
        table_term,
        spread(projection_sums[:part], (part,), 0),
        spread(projection_sums[2 * part :], (part,), 0),
        columns(branch_low),
        columns(upstream),
        first_gain_grad,
        first_shift_grad,
        second_gain_grad,
        second_shift_grad,
        spread(columns(upper_low), (size, units), 1),
    ]
    packed = jnp.concatenate([row.reshape(-1, width) for row in rows])
    used = packed.shape[0]
    packed = jnp.pad(packed, ((0, -used % 32), (0, 0)))
    total = sum_everywhere(packed)
    vectors = total[TABLE:used]
    return (
        block_out,
        embedded_grad.astype(bf16),
        total[:TABLE],
        input_weight_grad,
        vectors[0],
        vectors[1],
        output_weight_grad,
        vectors[2],
        up_weight_grad,
        vectors[8:].reshape(-1),
        down_weight_grad,
        vectors[3],
        vectors[4],
        vectors[5],
        vectors[6],
        vectors[7],
    )


def on_device(
    tokens,
    classes,
    source_index,
    position_table,
    input_weight,
    query_bias,
    value_bias,
    output_weight,
    output_bias,
    up_weight,
    up_bias,
    down_weight,
    down_bias,
    first_gain,
    first_shift,
    second_gain,
    second_shift,
    cotangent,
):
    if up_weight.shape[1] // lax.axis_size("img") // GROUP % 128:
        return generic_device(
            tokens,
            classes,
            source_index,
            position_table,
            input_weight,
            query_bias,
            value_bias,
            output_weight,
            output_bias,
            up_weight,
            up_bias,
            down_weight,
            down_bias,
            first_gain,
            first_shift,
            second_gain,
            second_shift,
            cotangent,
        )
    shard_rows, width = tokens.shape
    size = lax.axis_size("img")
    img, seq = lax.axis_index("img"), lax.axis_index("seq")
    held = width // size
    part = width // GROUP
    hidden_units = up_weight.shape[1]
    units = hidden_units // size // GROUP
    relatives = img ^ jnp.arange(size, dtype=jnp.int32)
    owners = seq ^ jnp.arange(GROUP, dtype=jnp.int32)
    seq_vector = seq[None].astype(jnp.int32)

    blocks = [(0, 1, t * width, 0, t * part, part) for t in range(2)]
    blocks += [(0, 1, 2 * width, 1, 0, part), (1, 1, 0, 1, part, part)]
    first_part, second_part = pick(
        [input_weight, output_weight], blocks, [(held, 2 * part)] * 2, seq_vector
    )
    first_parts = gather_relative(first_part)
    second_parts = gather_relative(second_part)
    blocks = [(0, 1, i * GROUP * units, 0, i * units, units) for i in range(size)]
    up_part, down_part = pick(
        [up_weight, down_weight],
        blocks + [(1, 0, 0, 1, 0, units)],
        [(held, size * units), (units, width)],
        seq_vector,
    )
    up_parts = gather_relative(up_part)
    down_parts = gather_relative(down_part)

    query_bias_part = mine_of(query_bias.reshape(GROUP, part), seq, 0)
    value_bias_part = mine_of(value_bias.reshape(GROUP, part), seq, 0)
    up_bias_part = mine_of(up_bias.reshape(size, GROUP, units), seq, 1).reshape(size * units)

    my_slots = seq * shard_rows + jnp.arange(shard_rows, dtype=jnp.int32)
    _, valid, mixing = table_mixing(classes, my_slots, source_index)
    all_slots = owners[:, None] * shard_rows + jnp.arange(shard_rows, dtype=jnp.int32)[None]
    all_segments, _ = slot_segments(classes, all_slots.reshape(-1))

    embedded = tokens.astype(f32) + jnp.dot(mixing, position_table, precision=highest)
    first_value, first_pull = jax.vjp(layer_norm, embedded, first_gain, first_shift)
    normed_all = jnp.concatenate(group_gather(first_value.astype(bf16)), axis=0)
    upstream = jnp.where(valid[:, None], cotangent.astype(f32), 0.0)
    upstream_all = jnp.concatenate(group_gather(upstream.astype(bf16)), axis=0)

    input_full, output_cols, queries, keys, values, attended, totals = attention_forward(
        relatives, normed_all, first_parts, second_parts, query_bias_part, value_bias_part, all_segments
    )
    attended = attended.reshape(GROUP * shard_rows, part)
    output_cols = output_cols.reshape(GROUP, part, part)
    output_blocks = [mine_of(output_cols, seq, 0)] + [
        exchange(mine_of(output_cols, seq ^ j, 0), "seq", j) for j in range(1, GROUP)
    ]
    output_full = jnp.concatenate(reorder(output_blocks, seq), axis=1)

    def row_parts(value):
        return [value[j * shard_rows : (j + 1) * shard_rows] for j in range(GROUP)]

    branch_one = group_scatter(
        row_parts(jnp.dot(attended, output_full, preferred_element_type=f32))
    )
    hidden = embedded + branch_one + output_bias
    second_value, second_pull = jax.vjp(layer_norm, hidden, second_gain, second_shift)
    second_rows = group_gather(second_value.astype(bf16))
    up_full, second_all, active, slope = feed_forward(relatives, second_rows, up_parts, up_bias_part)
    second_all = second_all.reshape(GROUP * shard_rows, width)
    active = active.reshape(GROUP * shard_rows, size * units)

    down_sum = scatter_pieces(weight_pieces(relatives, active, upstream_all))
    down_full, upper_low, upper_sums, sent, kept = feed_backward(
        relatives, upstream_all.reshape(GROUP, shard_rows, width), down_parts, slope, up_full
    )
    upper_low = upper_low.reshape(GROUP * shard_rows, size * units)
    beside = exchange(sent, "seq", 1)
    far = kept[0] + beside[0].astype(f32)
    second_grad = kept[1] + beside[1].astype(f32)
    second_grad += exchange(far.astype(bf16), "seq", 2).astype(f32)
    up_sum = scatter_pieces(weight_pieces(relatives, second_all, upper_low))
    branch_two = group_scatter(row_parts(jnp.dot(active, down_full, preferred_element_type=f32)))
    block_out = jnp.where(valid[:, None], hidden + branch_two + down_bias, 0.0).astype(bf16)

    hidden_grad, second_gain_grad, second_shift_grad = second_pull(second_grad)
    hidden_grad = hidden_grad + upstream
    branch_low = hidden_grad.astype(bf16)
    branch_all = jnp.concatenate(group_gather(branch_low), axis=0)
    mixed_grad = jnp.einsum("sd,cd->sc", branch_all, output_full, preferred_element_type=f32)
    projection_grad, projection_sums = attention_backward(
        queries, keys, values, mixed_grad.astype(bf16), totals, all_segments
    )
    projection_sums = projection_sums[0]

    term_blocks = group_terms(owners, attended, branch_all)
    term_blocks = [term_blocks[0]] + [exchange(term_blocks[j], "seq", j) for j in range(1, GROUP)]
    per_group = size // GROUP
    stacked = jnp.stack(term_blocks).reshape(size, held, part)
    pieces = [
        mine_of(stacked, ((img ^ j) // per_group ^ seq) * per_group + (img ^ j) % per_group, 0)
        for j in range(size)
    ]
    output_sum = scatter_pieces((jnp.stack(pieces[1::2]), jnp.stack(pieces[0::2]).astype(f32)))

    normed_grad = group_scatter(
        row_parts(jnp.einsum("se,de->sd", projection_grad, input_full, preferred_element_type=f32)),
    )
    input_sum = scatter_pieces(weight_pieces(relatives, normed_all, projection_grad))
    embedded_grad, first_gain_grad, first_shift_grad = first_pull(normed_grad)
    embedded_grad = embedded_grad + hidden_grad
    table_term = jnp.einsum("st,sd->td", mixing, embedded_grad, precision=highest)

    feed_shares = group_gather(jnp.stack([up_sum.astype(bf16), down_sum.astype(bf16)]))
    up_weight_grad = spread_columns(owners, [share[0] for share in feed_shares], size)
    down_weight_grad = spread_rows(owners, [share[1] for share in feed_shares])
    output_weight_grad = spread_columns(owners, group_gather(output_sum.astype(bf16)), 1)
    input_weight_grad = spread_columns(owners, group_gather(input_sum.astype(bf16)), 3)

    def spread(value, shape, axis):
        value = jnp.expand_dims(value.reshape(shape), axis)
        mask = jnp.arange(GROUP, dtype=jnp.int32).reshape([-1 if a == axis else 1 for a in range(value.ndim)])
        return jnp.where(mask == seq, value, 0.0).reshape(-1)

    def columns(value):
        return jnp.sum(value.astype(f32), axis=0)

    rows = [
        table_term,
        spread(projection_sums[:part], (part,), 0),
        spread(projection_sums[2 * part :], (part,), 0),
        columns(branch_low),
        columns(upstream),
        first_gain_grad,
        first_shift_grad,
        second_gain_grad,
        second_shift_grad,
        spread(upper_sums[0], (size, units), 1),
    ]
    packed = jnp.concatenate([row.reshape(-1, width) for row in rows])
    used = packed.shape[0]
    packed = jnp.pad(packed, ((0, -used % 32), (0, 0)))
    total = sum_everywhere(packed)
    vectors = total[TABLE:used]
    return (
        block_out,
        embedded_grad.astype(bf16),
        total[:TABLE],
        input_weight_grad,
        vectors[0],
        vectors[1],
        output_weight_grad,
        vectors[2],
        up_weight_grad,
        vectors[8:].reshape(-1),
        down_weight_grad,
        vectors[3],
        vectors[4],
        vectors[5],
        vectors[6],
        vectors[7],
    )


def solution(mesh):
    placed = (
        P(("img", "seq"), None),
        P("img"),
        P(),
        P(),
        P("img", None),
        P(),
        P(),
        P("img", None),
        P(),
        P("img", None),
        P(),
        P("img", None),
        P(),
        P(),
        P(),
        P(),
        P(),
        P(("img", "seq"), None),
    )
    return jax.shard_map(
        on_device,
        mesh=mesh,
        in_specs=placed,
        out_specs=(
            P(("img", "seq"), None),
            P(("img", "seq"), None),
            P(),
            P("img", None),
            P(),
            P(),
            P("img", None),
            P(),
            P("img", None),
            P(),
            P("img", None),
            P(),
            P(),
            P(),
            P(),
            P(),
        ),
        check_vma=False,
    )
```

```python
import jax
import jax.numpy as jnp
from jax import lax
from jax.experimental import pallas as pl
from jax.experimental.pallas import tpu as pltpu
from jax.sharding import PartitionSpec as P

HEADS = 16
HEAD_DIM = 64
TABLE = 50
LONG = 145
IMG_GRP = 4


highest = lax.Precision.HIGHEST
epsilon = 1e-06
masked_value = -1e30


def layer_norm(inputs, norm_gain, norm_shift):
    average = jnp.mean(inputs, axis=-1, keepdims=True)
    centred = inputs - average
    spread = jnp.mean(centred * centred, axis=-1, keepdims=True)
    return centred * lax.rsqrt(spread + epsilon) * norm_gain + norm_shift


def exact_gelu(inputs):
    return jax.nn.gelu(inputs, approximate=False)


def slot_segments(classes, slot_ids):
    counts = TABLE + (LONG - TABLE) * classes
    image_ends = jnp.cumsum(counts)
    segment = jnp.sum((slot_ids[:, None] >= image_ends[None, :]).astype(jnp.int32), axis=1)
    return (segment, image_ends - counts)


def table_mixing(classes, slot_ids, source_index):
    segment, starts = slot_segments(classes, slot_ids)
    images = jnp.arange(IMG_GRP, dtype=jnp.int32)
    picked = segment[:, None] == images[None, :]
    valid = segment < IMG_GRP
    start_of = jnp.sum(jnp.where(picked, starts[None, :], 0), axis=1)
    larger = jnp.sum(jnp.where(picked, classes[None, :], 0), axis=1) > 0
    place = jnp.where(valid, slot_ids - start_of, 0)
    columns = jnp.arange(TABLE, dtype=jnp.int32)
    direct = (place[:, None] == columns[None, :]).astype(jnp.float32)
    positions = jnp.arange(LONG, dtype=jnp.int32)
    sources = jnp.sum(
        jnp.where(place[:, None, None] == positions[None, :, None], source_index[None, :, :], 0),
        axis=1,
    )
    across = ((place * 7 % 12).astype(jnp.float32) + 0.5) / 12.0
    downward = ((place * 5 % 12).astype(jnp.float32) + 0.5) / 12.0
    corners = jnp.stack(
        [
            (1.0 - across) * (1.0 - downward),
            (1.0 - across) * downward,
            across * (1.0 - downward),
            across * downward,
        ],
        axis=1,
    )
    blended = jnp.sum(
        jnp.where(sources[:, :, None] == columns[None, None, :], corners[:, :, None], 0.0), axis=1
    )
    mixing = jnp.where(
        (valid & larger)[:, None], blended, jnp.where((valid & ~larger)[:, None], direct, 0.0)
    )
    return (segment, valid, mixing)


IMG, SEQ = "img", "seq"
GROUP = 4
f32 = jnp.float32
bf16 = jnp.bfloat16


def exchange(value, axis, distance):
    size = lax.axis_size(axis)
    return lax.ppermute(value, axis, [(i, i ^ distance) for i in range(size)])


def phases(size):
    found, stride = [], size
    while stride > 1:
        radix = 4 if stride % 4 == 0 else 2
        stride //= radix
        found.append((stride, radix))
    return found


def gather_relative(shard):
    parts = {0: shard}
    for stride, radix in phases(lax.axis_size(IMG)):
        held = dict(parts)
        if len(held) <= 4:
            for j, part in held.items():
                for digit in range(1, radix):
                    parts[j ^ (digit * stride)] = exchange(part, IMG, digit * stride)
        else:
            order = sorted(held)
            stacked = jnp.stack([held[j] for j in order])
            for digit in range(1, radix):
                received = exchange(stacked, IMG, digit * stride)
                for position, j in enumerate(order):
                    parts[j ^ (digit * stride)] = received[position]
    return [parts[j] for j in range(len(parts))]


def scatter_relative(pieces):
    held = {j: piece for j, piece in enumerate(pieces)}
    for stride, radix in reversed(phases(lax.axis_size(IMG))):
        keep = sorted(j for j in held if (j // stride) % radix == 0)
        total = {j: held[j] for j in keep}
        order = [j for j in keep if j != 0] + [0]
        if len(keep) <= 4:
            for j in order:
                for digit in range(1, radix):
                    sent = held[j + digit * stride].astype(bf16)
                    total[j] = total[j] + exchange(sent, IMG, digit * stride).astype(f32)
        else:
            for digit in range(1, radix):
                sent = jnp.stack([held[j + digit * stride].astype(bf16) for j in keep])
                received = exchange(sent, IMG, digit * stride)
                for position, j in enumerate(keep):
                    total[j] = total[j] + received[position].astype(f32)
        held = total
    return held[0]


def group_gather(value):
    across = exchange(value, SEQ, 2)
    beside = exchange(value, SEQ, 1)
    return [value, beside, across, exchange(across, SEQ, 1)]


def group_scatter(parts):
    sent = jnp.stack([parts[3], parts[1]]).astype(bf16)
    return group_total(sent, jnp.stack([parts[2], parts[0]]))


def group_total(sent, kept):
    beside = exchange(sent, SEQ, 1)
    far = kept[0] + beside[0].astype(f32)
    near = kept[1] + beside[1].astype(f32)
    return near + exchange(far.astype(bf16), SEQ, 2).astype(f32)


def place_kernel(count):
    def kernel(index_ref, *refs):
        for j in range(count):
            refs[count][index_ref[j]] = refs[j][...]

    return kernel


def place(parts, mine):
    count = len(parts)
    index = mine ^ jnp.arange(count, dtype=jnp.int32)
    return pl.pallas_call(
        place_kernel(count),
        out_shape=jax.ShapeDtypeStruct((count,) + parts[0].shape, parts[0].dtype),
        in_specs=[pl.BlockSpec(memory_space=pltpu.SMEM)]
        + [pl.BlockSpec(memory_space=pltpu.VMEM)] * count,
        out_specs=pl.BlockSpec(memory_space=pltpu.VMEM),
        name="place",
    )(index, *parts)


def sum_everywhere(value):
    rows = value.shape[0] // 2
    seq = lax.axis_index(SEQ)
    low, high = seq & 1, (seq >> 1) & 1
    halves = value.reshape(2, rows, -1)
    mine = mine_of(halves, low, 0) + exchange(mine_of(halves, 1 - low, 0), SEQ, 1)
    halves = mine.reshape(2, rows // 2, -1)
    mine = mine_of(halves, high, 0) + exchange(mine_of(halves, 1 - high, 0), SEQ, 2)
    for stride, radix in reversed(phases(lax.axis_size(IMG))):
        others = [mine] + [exchange(mine, IMG, digit * stride) for digit in range(1, radix)]
        while len(others) > 1:
            others = [others[i] + others[i + 1] for i in range(0, len(others), 2)]
        mine = others[0]
    other = exchange(mine, SEQ, 2)
    mine = jnp.where(high == 0, jnp.concatenate([mine, other]), jnp.concatenate([other, mine]))
    other = exchange(mine, SEQ, 1)
    return jnp.where(low == 0, jnp.concatenate([mine, other]), jnp.concatenate([other, mine]))


def reorder(parts, mine):
    stacked = jnp.stack(parts)
    return [lax.dynamic_index_in_dim(stacked, mine ^ p, 0, keepdims=False) for p in range(GROUP)]


def mine_of(array, mine, axis):
    return lax.dynamic_index_in_dim(array, mine, axis, keepdims=False)


VMEM = pl.BlockSpec(memory_space=pltpu.VMEM)
SMEM = pl.BlockSpec(memory_space=pltpu.SMEM)
ROWS = (((0,), (0,)), ((), ()))
LAST = (((1,), (1,)), ((), ()))


def local_call(kernel, outs, inputs, scratch=()):
    return pl.pallas_call(
        kernel,
        out_shape=[jax.ShapeDtypeStruct(shape, kind) for shape, kind in outs],
        in_specs=[SMEM] + [VMEM] * (len(inputs) - 1),
        out_specs=[VMEM] * len(outs),
        scratch_shapes=list(scratch),
        compiler_params=pltpu.CompilerParams(vmem_limit_bytes=56 * 1024 * 1024),
    )(*inputs)


def pick(sources, blocks, outs, index):
    count = len(blocks)

    def kernel(index_ref, *refs):
        ins, results, sems = refs[: len(sources)], refs[len(sources) : -1], refs[-1]
        copies = []
        for number, (source, axis, start, out, there, length) in enumerate(blocks):
            begin = pl.multiple_of(start + index_ref[0] * length, length)
            if axis == 0:
                origin, target = ins[source].at[pl.ds(begin, length), :], results[out]
            else:
                origin = ins[source].at[:, pl.ds(begin, length)]
                target = results[out].at[:, pl.ds(there, length)]
            copies.append(pltpu.make_async_copy(origin, target, sems.at[number]))
        for copy in copies:
            copy.start()
        for copy in copies:
            copy.wait()

    return pl.pallas_call(
        kernel,
        out_shape=[jax.ShapeDtypeStruct(shape, bf16) for shape in outs],
        in_specs=[SMEM] + [pl.BlockSpec(memory_space=pl.ANY)] * len(sources),
        out_specs=[VMEM] * len(outs),
        scratch_shapes=[pltpu.SemaphoreType.DMA((count,))],
    )(index, *sources)


def place_in(index_ref, parts, out, source, target):
    rows = parts[0].shape[0]
    for j, part in enumerate(parts):
        at = pl.ds(pl.multiple_of(index_ref[j] * rows, rows), rows)
        out[at, target[0] : target[1]] = part[:, source[0] : source[1]]


def attention_forward(index, normed, firsts, seconds, query_bias, value_bias, segments):
    slots, width = normed.shape
    part = width // GROUP
    heads = part // HEAD_DIM
    rows = slots // GROUP
    count = len(firsts)
    scale = HEAD_DIM ** (-0.5)

    def kernel(index_ref, x_ref, *refs):
        halves, refs = (refs[:count], refs[count : 2 * count]), refs[2 * count :]
        qb_ref, vb_ref, seg_rows, seg_cols = refs[:4]
        w_out, q_out, k_out, v_out, att_out, total_out = refs[4:]
        place_in(index_ref, halves[0], w_out, (0, 2 * part), (0, 2 * part))
        place_in(index_ref, halves[1], w_out, (0, part), (2 * part, 3 * part))
        projected = jnp.dot(x_ref[...], w_out[...], preferred_element_type=f32)
        queries = (projected[:, :part] + qb_ref[...]).astype(bf16)
        for block in range(GROUP):
            q_out[block] = queries[block * rows : (block + 1) * rows]
        k_out[...] = projected[:, part : 2 * part].astype(bf16)
        v_out[...] = (projected[:, 2 * part :] + vb_ref[...]).astype(bf16)

        def step(block, carry):
            same = seg_rows[block] == seg_cols[...]
            mixed, totals = [], []
            for h in range(heads):
                lanes = slice(h * HEAD_DIM, (h + 1) * HEAD_DIM)
                raw = lax.dot_general(
                    q_out[block, :, lanes], k_out[:, lanes], LAST, preferred_element_type=f32
                )
                logits = jnp.where(same, raw * scale, masked_value)
                top = jnp.max(logits, axis=-1, keepdims=True)
                raised = jnp.exp(logits - top)
                total = jnp.sum(raised, axis=-1, keepdims=True)
                probs = (raised * (1.0 / total)).astype(bf16)
                mixed.append(jnp.dot(probs, v_out[:, lanes], preferred_element_type=f32))
                totals.append(top + jnp.log(total))
            att_out[block] = jnp.concatenate(mixed, axis=1).astype(bf16)
            total_out[block] = jnp.concatenate(totals, axis=1)
            return carry

        lax.fori_loop(0, GROUP, step, 0)

    outs = [
        ((width, 3 * part), bf16),
        ((GROUP, rows, part), bf16),
        ((slots, part), bf16),
        ((slots, part), bf16),
        ((GROUP, rows, part), bf16),
        ((GROUP, rows, heads), f32),
    ]
    inputs = [index, normed, *firsts, *seconds, query_bias[None], value_bias[None]]
    inputs += [segments.reshape(GROUP, rows, 1), segments[None]]
    return local_call(kernel, outs, inputs)


def attention_backward(queries, keys, values, mixed_grad, totals, segments):
    blocks, rows, part = queries.shape
    slots = keys.shape[0]
    heads = part // HEAD_DIM
    scale = HEAD_DIM ** (-0.5)

    def kernel(zero_ref, q_ref, k_ref, v_ref, g_ref, t_ref, seg_rows, seg_cols, out, sums, acc):
        acc[...] = jnp.zeros_like(acc)

        def step(block, carry):
            same = seg_rows[block] == seg_cols[...]
            q_grads, k_grads, v_grads = [], [], []
            for h in range(heads):
                lanes = slice(h * HEAD_DIM, (h + 1) * HEAD_DIM)
                query, key, grad = q_ref[block, :, lanes], k_ref[:, lanes], g_ref[block, :, lanes]
                raw = lax.dot_general(query, key, LAST, preferred_element_type=f32)
                logits = jnp.where(same, raw * scale, masked_value)
                probs = jnp.exp(logits - t_ref[block, :, h : h + 1])
                probs_grad = lax.dot_general(
                    grad, v_ref[:, lanes], LAST, preferred_element_type=f32
                )
                weighted = probs * probs_grad
                inner = jnp.sum(weighted, axis=-1, keepdims=True)
                score = (scale * (weighted - probs * inner)).astype(bf16)
                q_grads.append(jnp.dot(score, key, preferred_element_type=f32))
                k_grads.append(
                    lax.dot_general(score, query, ROWS, preferred_element_type=f32)
                )
                v_grads.append(
                    lax.dot_general(probs.astype(bf16), grad, ROWS, preferred_element_type=f32)
                )
            start = pl.multiple_of(block * rows, 8)
            acc[pl.ds(start, rows), :part] = jnp.concatenate(q_grads, axis=1)
            acc[:, part:] += jnp.concatenate(k_grads + v_grads, axis=1)
            return carry

        lax.fori_loop(0, blocks, step, 0)
        rounded = acc[...].astype(bf16)
        out[...] = rounded
        sums[...] = jnp.sum(rounded.astype(f32), axis=0, keepdims=True)

    outs = [((slots, 3 * part), bf16), ((1, 3 * part), f32)]
    inputs = [jnp.zeros((1,), jnp.int32), queries, keys, values]
    inputs += [mixed_grad.reshape(blocks, rows, part), totals]
    inputs += [segments.reshape(blocks, rows, 1), segments[None]]
    scratch = [pltpu.VMEM((slots, 3 * part), f32)]
    return local_call(kernel, outs, inputs, scratch)


def feed_forward(index, seconds, parts, bias):
    rows, width = seconds[0].shape
    count, units = len(parts), parts[0].shape[1]
    half = 0.5**0.5

    def kernel(index_ref, *refs):
        xs, refs = refs[:GROUP], refs[GROUP:]
        weights, refs = refs[:count], refs[count:]
        b_ref, w_out, x_out, active_out, slope_out, upper = refs
        place_in(index_ref, weights, w_out, (0, units), (0, units))
        for j in range(GROUP):
            x_out[j] = xs[j][...]
            upper[...] = jnp.dot(xs[j][...], w_out[...], preferred_element_type=f32) + b_ref[...]

            def step(i, carry, j=j):
                at = pl.ds(pl.multiple_of(i * 8, 8), 8)
                u = upper[at, :]
                share = 0.5 * (1.0 + lax.erf(u * half))
                upper[at, :] = u * share
                slope_out[j, at, :] = share + u * jnp.exp(-0.5 * u * u) * 0.3989422804014327
                return carry

            lax.fori_loop(0, rows // 8, step, 0)
            active_out[j] = upper[...].astype(bf16)

    outs = [
        ((width, units), bf16),
        ((GROUP, rows, width), bf16),
        ((GROUP, rows, units), bf16),
        ((GROUP, rows, units), f32),
    ]
    inputs = [index, *seconds, *parts, bias[None]]
    return local_call(kernel, outs, inputs, [pltpu.VMEM((rows, units), f32)])


def feed_backward(index, upstream, parts, slope, up_full):
    blocks, rows, units = slope.shape
    width = upstream.shape[-1]
    count = len(parts)

    def kernel(index_ref, g_ref, *refs):
        weights, refs = refs[:count], refs[count:]
        s_ref, up_ref, w_out, upper_out, sums, sent, kept = refs
        place_in(index_ref, weights, w_out, (0, width), (0, width))
        for j in (3, 1, 2, 0):
            grad = lax.dot_general(g_ref[j], w_out[...], LAST, preferred_element_type=f32)
            low = (grad * s_ref[j]).astype(bf16)
            upper_out[j] = low
            total = jnp.sum(low.astype(f32), axis=0, keepdims=True)
            sums[...] = total if j == 3 else sums[...] + total
            back = lax.dot_general(low, up_ref[...], LAST, preferred_element_type=f32)
            if j % 2:
                sent[(3 - j) // 2] = back.astype(bf16)
            else:
                kept[(2 - j) // 2] = back

    outs = [
        ((count * parts[0].shape[0], width), bf16),
        ((blocks, rows, units), bf16),
        ((1, units), f32),
        ((2, rows, width), bf16),
        ((2, rows, width), f32),
    ]
    return local_call(kernel, outs, [index, upstream, *parts, slope, up_full])


def weight_pieces(index, left, right):
    count = index.shape[0]
    rows = left.shape[1] // count
    shape = (count // 2, rows, right.shape[1])

    def kernel(index_ref, left_ref, right_ref, sent, kept):
        for j in [*range(1, count, 2), *range(0, count, 2)]:
            block = left_ref[:, pl.ds(pl.multiple_of(index_ref[j] * rows, rows), rows)]
            term = lax.dot_general(block, right_ref[...], ROWS, preferred_element_type=f32)
            if j % 2:
                sent[j // 2] = term.astype(bf16)
            else:
                kept[j // 2] = term

    return local_call(kernel, [(shape, bf16), (shape, f32)], [index, left, right])


def group_terms(owners, left, right):
    columns = right.shape[1] // GROUP

    def kernel(owner_ref, left_ref, right_ref, *outs):
        for j in range(GROUP):
            start = pl.multiple_of(owner_ref[j] * columns, columns)
            block = right_ref[:, pl.ds(start, columns)]
            term = lax.dot_general(left_ref[...], block, ROWS, preferred_element_type=f32)
            outs[j][...] = term.astype(bf16)

    shape = ((left.shape[1], columns), bf16)
    return local_call(kernel, [shape] * GROUP, [owners, left, right])


def fold(kept, received):
    count, rows, columns = kept.shape

    def kernel(zero_ref, kept_ref, received_ref, own, *sent):
        for digit in range(1, count):
            sent[digit - 1][...] = (kept_ref[digit] + received_ref[digit].astype(f32)).astype(bf16)
        own[...] = kept_ref[0] + received_ref[0].astype(f32)

    outs = [((rows, columns), f32)] + [((rows, columns), bf16)] * (count - 1)
    return local_call(kernel, outs, [jnp.zeros((1,), jnp.int32), kept, received])


def finish(groups):
    sizes = [len(group) for group in groups]
    widths = [group[0].shape[1] for group in groups]
    rows = groups[0][0].shape[0]

    def kernel(zero_ref, *refs):
        refs, out = refs[:-1], refs[-1]
        start = column = 0
        for size, columns in zip(sizes, widths):
            total = refs[start][...]
            for other in refs[start + 1 : start + size]:
                total = total + other[...].astype(f32)
            out[:, column : column + columns] = total.astype(bf16)
            start, column = start + size, column + columns

    inputs = [jnp.zeros((1,), jnp.int32)] + [value for group in groups for value in group]
    return local_call(kernel, [((rows, sum(widths)), bf16)], inputs)[0]


def scatter_pieces(pieces):
    sent, kept = pieces
    own, *others = fold(kept, exchange(sent, IMG, 1))
    return [own] + [exchange(other, IMG, 2 * digit) for digit, other in enumerate(others, 1)]


def row_halves(left, right, transposed):
    _, rows = left.shape[:2]
    columns = right.shape[0 if transposed else 1]
    dims = LAST if transposed else (((1,), (0,)), ((), ()))

    def kernel(zero_ref, left_ref, right_ref, sent, kept):
        for j in (3, 1, 2, 0):
            value = lax.dot_general(left_ref[j], right_ref[...], dims, preferred_element_type=f32)
            if j % 2:
                sent[(3 - j) // 2] = value.astype(bf16)
            else:
                kept[(2 - j) // 2] = value

    outs = [((2, rows, columns), bf16), ((2, rows, columns), f32)]
    return local_call(kernel, outs, [jnp.zeros((1,), jnp.int32), left, right])


def add_far(kept, beside):
    def kernel(zero_ref, kept_ref, beside_ref, out):
        out[...] = (kept_ref[0] + beside_ref[0].astype(f32)).astype(bf16)

    inputs = [jnp.zeros((1,), jnp.int32), kept, beside]
    return local_call(kernel, [(kept.shape[1:], bf16)], inputs)[0]


def block_end(kept, beside, moved, hidden, bias, valid):
    def kernel(zero_ref, kept_ref, beside_ref, moved_ref, hidden_ref, bias_ref, valid_ref, out):
        branch = kept_ref[1] + beside_ref[1].astype(f32) + moved_ref[...].astype(f32)
        value = hidden_ref[...] + branch + bias_ref[...]
        out[...] = jnp.where(valid_ref[...] > 0, value, 0.0).astype(bf16)

    inputs = [jnp.zeros((1,), jnp.int32), kept, beside, moved, hidden, bias[None]]
    inputs.append(valid[:, None].astype(f32))
    return local_call(kernel, [(hidden.shape, bf16)], inputs)[0]


def output_places(index, seq_vector, parts):
    rows, columns = parts[0].shape
    size = columns // 2
    per_group = len(parts) // GROUP

    def kernel(index_ref, seq_ref, *refs):
        out = refs[-1]
        for j in range(len(parts)):
            group, place = index_ref[j] // per_group, index_ref[j] % per_group
            at = pl.ds(pl.multiple_of(place * rows, rows), rows)
            out[group ^ seq_ref[0], at, :] = refs[j][:, size:]

    return pl.pallas_call(
        kernel,
        out_shape=jax.ShapeDtypeStruct((GROUP, per_group * rows, size), bf16),
        in_specs=[SMEM, SMEM] + [VMEM] * len(parts),
        out_specs=VMEM,
    )(index, seq_vector, *parts)


def branch_halves(owners, attended, blocks):
    _, rows, part = attended.shape
    width = part * GROUP

    def kernel(owner_ref, a_ref, *refs):
        parts, (w_out, sent, kept) = refs[:GROUP], refs[GROUP:]
        for k in range(GROUP):
            w_out[:, pl.ds(pl.multiple_of(owner_ref[k] * part, part), part)] = parts[k][...]
        for j in (3, 1, 2, 0):
            value = jnp.dot(a_ref[j], w_out[...], preferred_element_type=f32)
            if j % 2:
                sent[(3 - j) // 2] = value.astype(bf16)
            else:
                kept[(2 - j) // 2] = value

    outs = [((part, width), bf16), ((2, rows, width), bf16), ((2, rows, width), f32)]
    return local_call(kernel, outs, [owners, attended, *blocks])


def spread_columns(owners, parts, repeats):
    rows, total = parts[0].shape
    size = total // sum(repeats)

    def kernel(owner_ref, *refs):
        for j in range(GROUP):
            column = 0
            for out, count in zip(refs[GROUP:], repeats):
                for r in range(count):
                    start = pl.multiple_of((r * GROUP + owner_ref[j]) * size, size)
                    out[:, pl.ds(start, size)] = refs[j][:, column : column + size].astype(f32)
                    column += size

    outs = [((rows, count * GROUP * size), f32) for count in repeats]
    return local_call(kernel, outs, [owners, *parts])


def spread_rows(owners, parts):
    rows, columns = parts[0].shape

    def kernel(owner_ref, *refs):
        for j in range(GROUP):
            start = pl.multiple_of(owner_ref[j] * rows, rows)
            refs[GROUP][pl.ds(start, rows), :] = refs[j][...].astype(f32)

    return local_call(kernel, [((rows * GROUP, columns), f32)], [owners, *parts])[0]


def generic_device(
    tokens,
    classes,
    source_index,
    position_table,
    input_weight,
    query_bias,
    value_bias,
    output_weight,
    output_bias,
    up_weight,
    up_bias,
    down_weight,
    down_bias,
    first_gain,
    first_shift,
    second_gain,
    second_shift,
    cotangent,
):
    shard_rows, width = tokens.shape
    group_slots = shard_rows * GROUP
    size = lax.axis_size(IMG)
    img, seq = lax.axis_index(IMG), lax.axis_index(SEQ)
    held = width // size
    part = width // GROUP
    heads = HEADS // GROUP
    hidden_units = up_weight.shape[1]
    units = hidden_units // size // GROUP
    scale = HEAD_DIM ** (-0.5)

    input_part = mine_of(input_weight.reshape(held, 3, GROUP, part), seq, 2).reshape(held, 3 * part)
    output_part = mine_of(output_weight.reshape(held, GROUP, part), seq, 1)
    up_part = mine_of(up_weight.reshape(held, size, GROUP, units), seq, 2).reshape(held, size * units)
    down_part = mine_of(down_weight.reshape(GROUP, units, width), seq, 0)
    input_full = place(gather_relative(input_part), img).reshape(width, 3 * part)
    output_cols = place(gather_relative(output_part), img).reshape(GROUP, part, part)
    up_full = place(gather_relative(up_part), img).reshape(width, size * units)
    down_full = place(gather_relative(down_part), img).reshape(size * units, width)
    output_blocks = [mine_of(output_cols, seq, 0)] + [
        exchange(mine_of(output_cols, seq ^ j, 0), SEQ, j) for j in range(1, GROUP)
    ]
    output_full = jnp.concatenate(reorder(output_blocks, seq), axis=1)
    query_bias_part = mine_of(query_bias.reshape(GROUP, part), seq, 0)
    value_bias_part = mine_of(value_bias.reshape(GROUP, part), seq, 0)
    up_bias_part = mine_of(up_bias.reshape(size, GROUP, units), seq, 1).reshape(size * units)

    my_slots = seq * shard_rows + jnp.arange(shard_rows, dtype=jnp.int32)
    _, valid, mixing = table_mixing(classes, my_slots, source_index)
    owners = seq ^ jnp.arange(GROUP, dtype=jnp.int32)
    all_slots = (owners[:, None] * shard_rows + jnp.arange(shard_rows, dtype=jnp.int32)[None]).reshape(-1)
    all_segments, _ = slot_segments(classes, all_slots)
    same_image = all_segments[:, None] == all_segments[None, :]

    upstream = jnp.where(valid[:, None], cotangent.astype(f32), 0.0)
    upstream_all = jnp.concatenate(group_gather(upstream.astype(bf16)), axis=0)

    embedded = tokens.astype(f32) + jnp.dot(mixing, position_table, precision=highest)
    first_value, first_pull = jax.vjp(layer_norm, embedded, first_gain, first_shift)
    normed_all = jnp.concatenate(group_gather(first_value.astype(bf16)), axis=0)
    projected = jnp.dot(normed_all, input_full, preferred_element_type=f32)

    def split_heads(value):
        return value.astype(bf16).reshape(group_slots, heads, HEAD_DIM)

    queries = split_heads(projected[:, :part] + query_bias_part)
    keys = split_heads(projected[:, part : 2 * part])
    values = split_heads(projected[:, 2 * part :] + value_bias_part)
    raw_scores = jnp.einsum("qhd,khd->hqk", queries, keys, preferred_element_type=f32)
    logits = jnp.where(same_image[None], raw_scores * scale, masked_value)
    row_max = jnp.max(logits, axis=-1, keepdims=True)
    log_total = row_max + jnp.log(jnp.sum(jnp.exp(logits - row_max), axis=-1, keepdims=True))
    probs = jnp.exp(logits - log_total)
    probs_low = probs.astype(bf16)
    attended = (
        jnp.einsum("hqk,khd->qhd", probs_low, values, preferred_element_type=f32)
        .reshape(group_slots, part)
        .astype(bf16)
    )

    def row_parts(value):
        return [value[j * shard_rows : (j + 1) * shard_rows] for j in range(GROUP)]

    branch_one = group_scatter(row_parts(jnp.dot(attended, output_full, preferred_element_type=f32)))
    hidden = embedded + branch_one + output_bias
    second_value, second_pull = jax.vjp(layer_norm, hidden, second_gain, second_shift)
    second_all = jnp.concatenate(group_gather(second_value.astype(bf16)), axis=0)
    upper = jnp.dot(second_all, up_full, preferred_element_type=f32) + up_bias_part
    active, gelu_pull = jax.vjp(exact_gelu, upper)
    active_low = active.astype(bf16)

    def to_owners(term, rows):
        pieces = term.reshape(size, rows, term.shape[1])
        return scatter_relative([mine_of(pieces, img ^ j, 0) for j in range(size)])

    def columns_of_all(total):
        return reorder(group_gather(total.astype(bf16)), seq)

    down_sum = to_owners(
        jnp.einsum("sf,sd->fd", active_low, upstream_all, preferred_element_type=f32), units
    )
    active_grad = jnp.einsum("sd,fd->sf", upstream_all, down_full, preferred_element_type=f32)
    upper_low = gelu_pull(active_grad)[0].astype(bf16)
    second_grad = group_scatter(
        row_parts(jnp.einsum("sf,df->sd", upper_low, up_full, preferred_element_type=f32))
    )
    up_sum = to_owners(
        jnp.einsum("sd,sf->df", second_all, upper_low, preferred_element_type=f32), held
    )
    branch_two = group_scatter(row_parts(jnp.dot(active_low, down_full, preferred_element_type=f32)))
    block_out = jnp.where(valid[:, None], hidden + branch_two + down_bias, 0.0).astype(bf16)

    hidden_grad, second_gain_grad, second_shift_grad = second_pull(second_grad)
    hidden_grad = hidden_grad + upstream
    branch_low = hidden_grad.astype(bf16)
    branch_all = jnp.concatenate(group_gather(branch_low), axis=0)
    output_term = jnp.einsum("sc,sd->cd", attended, branch_all, preferred_element_type=f32)
    output_term = output_term.astype(bf16).reshape(part, GROUP, part)
    term_blocks = [mine_of(output_term, seq, 1)] + [
        exchange(mine_of(output_term, seq ^ j, 1), SEQ, j) for j in range(1, GROUP)
    ]
    output_sum = to_owners(jnp.concatenate(reorder(term_blocks, seq), axis=0).astype(f32), held)

    attended_grad = jnp.einsum(
        "sd,cd->sc", branch_all, output_full, preferred_element_type=f32
    )
    attended_grad = split_heads(attended_grad)
    probs_grad = jnp.einsum("qhd,khd->hqk", attended_grad, values, preferred_element_type=f32)
    inner = jnp.sum(probs * probs_grad, axis=-1, keepdims=True)
    score_low = (scale * (probs * (probs_grad - inner))).astype(bf16)
    query_grad = jnp.einsum("hqk,khd->qhd", score_low, keys, preferred_element_type=f32)
    key_grad = jnp.einsum("hqk,qhd->khd", score_low, queries, preferred_element_type=f32)
    value_grad = jnp.einsum("hqk,qhd->khd", probs_low, attended_grad, preferred_element_type=f32)
    projection_grad = jnp.concatenate(
        [grad.reshape(group_slots, part).astype(bf16) for grad in (query_grad, key_grad, value_grad)],
        axis=1,
    )
    input_sum = to_owners(
        jnp.einsum("sd,se->de", normed_all, projection_grad, preferred_element_type=f32), held
    )
    normed_grad = group_scatter(
        row_parts(jnp.einsum("se,de->sd", projection_grad, input_full, preferred_element_type=f32))
    )
    embedded_grad, first_gain_grad, first_shift_grad = first_pull(normed_grad)
    embedded_grad = embedded_grad + hidden_grad
    table_term = jnp.einsum("st,sd->td", mixing, embedded_grad, precision=highest)

    input_columns = [c.reshape(held, 3, part) for c in columns_of_all(input_sum)]
    input_weight_grad = jnp.stack(input_columns, axis=2).reshape(held, 3 * width).astype(f32)
    output_weight_grad = jnp.concatenate(columns_of_all(output_sum), axis=1).astype(f32)
    up_columns = [c.reshape(held, size, units) for c in columns_of_all(up_sum)]
    up_weight_grad = jnp.stack(up_columns, axis=2).reshape(held, hidden_units).astype(f32)
    down_weight_grad = jnp.concatenate(columns_of_all(down_sum), axis=0).astype(f32)

    def spread(value, shape, axis):
        value = jnp.expand_dims(value.reshape(shape), axis)
        mask = jnp.arange(GROUP, dtype=jnp.int32).reshape([-1 if a == axis else 1 for a in range(value.ndim)])
        return jnp.where(mask == seq, value, 0.0).reshape(-1)

    def columns(value):
        return jnp.sum(value.astype(f32), axis=0)

    projection_sums = columns(projection_grad)
    rows = [
        table_term,
        spread(projection_sums[:part], (part,), 0),
        spread(projection_sums[2 * part :], (part,), 0),
        columns(branch_low),
        columns(upstream),
        first_gain_grad,
        first_shift_grad,
        second_gain_grad,
        second_shift_grad,
        spread(columns(upper_low), (size, units), 1),
    ]
    packed = jnp.concatenate([row.reshape(-1, width) for row in rows])
    used = packed.shape[0]
    packed = jnp.pad(packed, ((0, -used % 32), (0, 0)))
    total = sum_everywhere(packed)
    vectors = total[TABLE:used]
    return (
        block_out,
        embedded_grad.astype(bf16),
        total[:TABLE],
        input_weight_grad,
        vectors[0],
        vectors[1],
        output_weight_grad,
        vectors[2],
        up_weight_grad,
        vectors[8:].reshape(-1),
        down_weight_grad,
        vectors[3],
        vectors[4],
        vectors[5],
        vectors[6],
        vectors[7],
    )


def on_device(
    tokens,
    classes,
    source_index,
    position_table,
    input_weight,
    query_bias,
    value_bias,
    output_weight,
    output_bias,
    up_weight,
    up_bias,
    down_weight,
    down_bias,
    first_gain,
    first_shift,
    second_gain,
    second_shift,
    cotangent,
):
    if up_weight.shape[1] // lax.axis_size(IMG) // GROUP % 128:
        return generic_device(
            tokens,
            classes,
            source_index,
            position_table,
            input_weight,
            query_bias,
            value_bias,
            output_weight,
            output_bias,
            up_weight,
            up_bias,
            down_weight,
            down_bias,
            first_gain,
            first_shift,
            second_gain,
            second_shift,
            cotangent,
        )
    shard_rows, width = tokens.shape
    size = lax.axis_size(IMG)
    img, seq = lax.axis_index(IMG), lax.axis_index(SEQ)
    held = width // size
    part = width // GROUP
    hidden_units = up_weight.shape[1]
    units = hidden_units // size // GROUP
    relatives = img ^ jnp.arange(size, dtype=jnp.int32)
    owners = seq ^ jnp.arange(GROUP, dtype=jnp.int32)
    seq_vector = seq[None].astype(jnp.int32)

    blocks = [(0, 1, t * width, 0, t * part, part) for t in range(2)]
    blocks += [(0, 1, 2 * width, 1, 0, part), (1, 1, 0, 1, part, part)]
    first_part, second_part = pick(
        [input_weight, output_weight], blocks, [(held, 2 * part)] * 2, seq_vector
    )
    first_parts = gather_relative(first_part)
    second_parts = gather_relative(second_part)
    blocks = [(0, 1, i * GROUP * units, 0, i * units, units) for i in range(size)]
    up_part, down_part = pick(
        [up_weight, down_weight],
        blocks + [(1, 0, 0, 1, 0, units)],
        [(held, size * units), (units, width)],
        seq_vector,
    )
    up_parts = gather_relative(up_part)
    down_parts = gather_relative(down_part)

    query_bias_part = mine_of(query_bias.reshape(GROUP, part), seq, 0)
    value_bias_part = mine_of(value_bias.reshape(GROUP, part), seq, 0)
    up_bias_part = mine_of(up_bias.reshape(size, GROUP, units), seq, 1).reshape(size * units)

    my_slots = seq * shard_rows + jnp.arange(shard_rows, dtype=jnp.int32)
    _, valid, mixing = table_mixing(classes, my_slots, source_index)
    all_slots = owners[:, None] * shard_rows + jnp.arange(shard_rows, dtype=jnp.int32)[None]
    all_segments, _ = slot_segments(classes, all_slots.reshape(-1))

    embedded = tokens.astype(f32) + jnp.dot(mixing, position_table, precision=highest)
    first_value, first_pull = jax.vjp(layer_norm, embedded, first_gain, first_shift)
    normed_all = jnp.concatenate(group_gather(first_value.astype(bf16)), axis=0)
    upstream = jnp.where(valid[:, None], cotangent.astype(f32), 0.0)
    upstream_all = jnp.concatenate(group_gather(upstream.astype(bf16)), axis=0)

    columns_of = output_places(relatives, seq_vector, second_parts)
    output_blocks = [columns_of[0]] + [exchange(columns_of[j], SEQ, j) for j in range(1, GROUP)]
    input_full, queries, keys, values, attended, totals = attention_forward(
        relatives, normed_all, first_parts, second_parts, query_bias_part, value_bias_part, all_segments
    )
    output_full, sent, kept = branch_halves(owners, attended, output_blocks)
    attended = attended.reshape(GROUP * shard_rows, part)
    branch_one = group_total(sent, kept)
    hidden = embedded + branch_one + output_bias
    second_value, second_pull = jax.vjp(layer_norm, hidden, second_gain, second_shift)
    second_rows = group_gather(second_value.astype(bf16))
    up_full, second_all, active, slope = feed_forward(relatives, second_rows, up_parts, up_bias_part)
    second_all = second_all.reshape(GROUP * shard_rows, width)
    flat_active = active.reshape(GROUP * shard_rows, size * units)
    down_sum = scatter_pieces(weight_pieces(relatives, flat_active, upstream_all))
    down_full, upper_low, upper_sums, sent, kept = feed_backward(
        relatives, upstream_all.reshape(GROUP, shard_rows, width), down_parts, slope, up_full
    )
    upper_low = upper_low.reshape(GROUP * shard_rows, size * units)
    second_grad = group_total(sent, kept)
    up_sum = scatter_pieces(weight_pieces(relatives, second_all, upper_low))
    sent, kept = row_halves(active, down_full, False)
    beside = exchange(sent, SEQ, 1)
    far = add_far(kept, beside)
    moved = exchange(far, SEQ, 2)
    block_out = block_end(kept, beside, moved, hidden, down_bias, valid)

    hidden_grad, second_gain_grad, second_shift_grad = second_pull(second_grad)
    hidden_grad = hidden_grad + upstream
    branch_low = hidden_grad.astype(bf16)
    branch_all = jnp.concatenate(group_gather(branch_low), axis=0)
    mixed_grad = jnp.einsum("sd,cd->sc", branch_all, output_full, preferred_element_type=f32)
    projection_grad, projection_sums = attention_backward(
        queries, keys, values, mixed_grad.astype(bf16), totals, all_segments
    )
    projection_sums = projection_sums[0]

    term_blocks = group_terms(owners, attended, branch_all)
    term_blocks = [term_blocks[0]] + [exchange(term_blocks[j], SEQ, j) for j in range(1, GROUP)]
    per_group = size // GROUP
    stacked = jnp.stack(term_blocks).reshape(size, held, part)
    pieces = [
        mine_of(stacked, ((img ^ j) // per_group ^ seq) * per_group + (img ^ j) % per_group, 0)
        for j in range(size)
    ]
    output_sum = scatter_pieces((jnp.stack(pieces[1::2]), jnp.stack(pieces[0::2]).astype(f32)))
    input_sum = scatter_pieces(weight_pieces(relatives, normed_all, projection_grad))
    row_grads = projection_grad.reshape(GROUP, shard_rows, 3 * part)
    normed_grad = group_total(*row_halves(row_grads, input_full, True))
    embedded_grad, first_gain_grad, first_shift_grad = first_pull(normed_grad)
    embedded_grad = embedded_grad + hidden_grad
    table_term = jnp.einsum("st,sd->td", mixing, embedded_grad, precision=highest)

    up_shares = group_gather(finish([up_sum]))
    down_shares = group_gather(finish([down_sum]))
    last_shares = group_gather(finish([input_sum, output_sum]))
    up_weight_grad = spread_columns(owners, up_shares, [size])[0]
    down_weight_grad = spread_rows(owners, down_shares)
    input_weight_grad, output_weight_grad = spread_columns(owners, last_shares, [3, 1])

    def spread(value, shape, axis):
        value = jnp.expand_dims(value.reshape(shape), axis)
        mask = jnp.arange(GROUP, dtype=jnp.int32).reshape([-1 if a == axis else 1 for a in range(value.ndim)])
        return jnp.where(mask == seq, value, 0.0).reshape(-1)

    def columns(value):
        return jnp.sum(value.astype(f32), axis=0)

    rows = [
        table_term,
        spread(projection_sums[:part], (part,), 0),
        spread(projection_sums[2 * part :], (part,), 0),
        columns(branch_low),
        columns(upstream),
        first_gain_grad,
        first_shift_grad,
        second_gain_grad,
        second_shift_grad,
        spread(upper_sums[0], (size, units), 1),
    ]
    packed = jnp.concatenate([row.reshape(-1, width) for row in rows])
    used = packed.shape[0]
    packed = jnp.pad(packed, ((0, -used % 32), (0, 0)))
    total = sum_everywhere(packed)
    vectors = total[TABLE:used]
    return (
        block_out,
        embedded_grad.astype(bf16),
        total[:TABLE],
        input_weight_grad,
        vectors[0],
        vectors[1],
        output_weight_grad,
        vectors[2],
        up_weight_grad,
        vectors[8:].reshape(-1),
        down_weight_grad,
        vectors[3],
        vectors[4],
        vectors[5],
        vectors[6],
        vectors[7],
    )


def solution(mesh):
    placed = (
        P((IMG, SEQ), None),
        P(IMG),
        P(),
        P(),
        P(IMG, None),
        P(),
        P(),
        P(IMG, None),
        P(),
        P(IMG, None),
        P(),
        P(IMG, None),
        P(),
        P(),
        P(),
        P(),
        P(),
        P((IMG, SEQ), None),
    )
    return jax.shard_map(
        on_device,
        mesh=mesh,
        in_specs=placed,
        out_specs=(
            P((IMG, SEQ), None),
            P((IMG, SEQ), None),
            P(),
            P(IMG, None),
            P(),
            P(),
            P(IMG, None),
            P(),
            P(IMG, None),
            P(),
            P(IMG, None),
            P(),
            P(),
            P(),
            P(),
            P(),
        ),
        check_vma=False,
    )
```

```python
import jax
import jax.numpy as jnp
from jax import lax
from jax.experimental import pallas as pl
from jax.experimental.pallas import tpu as pltpu
from jax.sharding import PartitionSpec as P

HEADS = 16
HEAD_DIM = 64
TABLE = 50
LONG = 145
IMG_GRP = 4


highest = lax.Precision.HIGHEST
epsilon = 1e-06
masked_value = -1e30


def layer_norm(inputs, norm_gain, norm_shift):
    average = jnp.mean(inputs, axis=-1, keepdims=True)
    centred = inputs - average
    spread = jnp.mean(centred * centred, axis=-1, keepdims=True)
    return centred * lax.rsqrt(spread + epsilon) * norm_gain + norm_shift


def exact_gelu(inputs):
    return jax.nn.gelu(inputs, approximate=False)


def slot_segments(classes, slot_ids):
    counts = TABLE + (LONG - TABLE) * classes
    image_ends = jnp.cumsum(counts)
    segment = jnp.sum((slot_ids[:, None] >= image_ends[None, :]).astype(jnp.int32), axis=1)
    return (segment, image_ends - counts)


def table_mixing(classes, slot_ids, source_index):
    segment, starts = slot_segments(classes, slot_ids)
    images = jnp.arange(IMG_GRP, dtype=jnp.int32)
    picked = segment[:, None] == images[None, :]
    valid = segment < IMG_GRP
    start_of = jnp.sum(jnp.where(picked, starts[None, :], 0), axis=1)
    larger = jnp.sum(jnp.where(picked, classes[None, :], 0), axis=1) > 0
    place = jnp.where(valid, slot_ids - start_of, 0)
    columns = jnp.arange(TABLE, dtype=jnp.int32)
    direct = (place[:, None] == columns[None, :]).astype(jnp.float32)
    positions = jnp.arange(LONG, dtype=jnp.int32)
    sources = jnp.sum(
        jnp.where(place[:, None, None] == positions[None, :, None], source_index[None, :, :], 0),
        axis=1,
    )
    across = ((place * 7 % 12).astype(jnp.float32) + 0.5) / 12.0
    downward = ((place * 5 % 12).astype(jnp.float32) + 0.5) / 12.0
    corners = jnp.stack(
        [
            (1.0 - across) * (1.0 - downward),
            (1.0 - across) * downward,
            across * (1.0 - downward),
            across * downward,
        ],
        axis=1,
    )
    blended = jnp.sum(
        jnp.where(sources[:, :, None] == columns[None, None, :], corners[:, :, None], 0.0), axis=1
    )
    mixing = jnp.where(
        (valid & larger)[:, None], blended, jnp.where((valid & ~larger)[:, None], direct, 0.0)
    )
    return (segment, valid, mixing)


IMG, SEQ = "img", "seq"
GROUP = 4
f32 = jnp.float32
bf16 = jnp.bfloat16


def exchange(value, axis, distance):
    size = lax.axis_size(axis)
    return lax.ppermute(value, axis, [(i, i ^ distance) for i in range(size)])


def phases(size):
    found, stride = [], size
    while stride > 1:
        radix = 4 if stride % 4 == 0 else 2
        stride //= radix
        found.append((stride, radix))
    return found


def gather_relative(shard):
    parts = {0: shard}
    for stride, radix in phases(lax.axis_size(IMG)):
        held = dict(parts)
        if len(held) <= 4:
            for j, part in held.items():
                for digit in range(1, radix):
                    parts[j ^ (digit * stride)] = exchange(part, IMG, digit * stride)
        else:
            order = sorted(held)
            stacked = jnp.stack([held[j] for j in order])
            for digit in range(1, radix):
                received = exchange(stacked, IMG, digit * stride)
                for position, j in enumerate(order):
                    parts[j ^ (digit * stride)] = received[position]
    return [parts[j] for j in range(len(parts))]


def scatter_relative(pieces):
    held = {j: piece for j, piece in enumerate(pieces)}
    for stride, radix in reversed(phases(lax.axis_size(IMG))):
        keep = sorted(j for j in held if (j // stride) % radix == 0)
        total = {j: held[j] for j in keep}
        order = [j for j in keep if j != 0] + [0]
        if len(keep) <= 4:
            for j in order:
                for digit in range(1, radix):
                    sent = held[j + digit * stride].astype(bf16)
                    total[j] = total[j] + exchange(sent, IMG, digit * stride).astype(f32)
        else:
            for digit in range(1, radix):
                sent = jnp.stack([held[j + digit * stride].astype(bf16) for j in keep])
                received = exchange(sent, IMG, digit * stride)
                for position, j in enumerate(keep):
                    total[j] = total[j] + received[position].astype(f32)
        held = total
    return held[0]


def group_gather(value):
    across = exchange(value, SEQ, 2)
    beside = exchange(value, SEQ, 1)
    return [value, beside, across, exchange(across, SEQ, 1)]


def group_scatter(parts):
    sent = jnp.stack([parts[3], parts[1]]).astype(bf16)
    return group_total(sent, jnp.stack([parts[2], parts[0]]))


def group_total(sent, kept):
    beside = exchange(sent, SEQ, 1)
    far = kept[0] + beside[0].astype(f32)
    near = kept[1] + beside[1].astype(f32)
    return near + exchange(far.astype(bf16), SEQ, 2).astype(f32)


def place_kernel(count):
    def kernel(index_ref, *refs):
        for j in range(count):
            refs[count][index_ref[j]] = refs[j][...]

    return kernel


def place(parts, mine):
    count = len(parts)
    index = mine ^ jnp.arange(count, dtype=jnp.int32)
    return pl.pallas_call(
        place_kernel(count),
        out_shape=jax.ShapeDtypeStruct((count,) + parts[0].shape, parts[0].dtype),
        in_specs=[pl.BlockSpec(memory_space=pltpu.SMEM)]
        + [pl.BlockSpec(memory_space=pltpu.VMEM)] * count,
        out_specs=pl.BlockSpec(memory_space=pltpu.VMEM),
        name="place",
    )(index, *parts)


def sum_everywhere(value):
    rows = value.shape[0] // 2
    seq = lax.axis_index(SEQ)
    low, high = seq & 1, (seq >> 1) & 1
    halves = value.reshape(2, rows, -1)
    mine = mine_of(halves, low, 0) + exchange(mine_of(halves, 1 - low, 0), SEQ, 1)
    halves = mine.reshape(2, rows // 2, -1)
    mine = mine_of(halves, high, 0) + exchange(mine_of(halves, 1 - high, 0), SEQ, 2)
    for stride, radix in reversed(phases(lax.axis_size(IMG))):
        others = [mine] + [exchange(mine, IMG, digit * stride) for digit in range(1, radix)]
        while len(others) > 1:
            others = [others[i] + others[i + 1] for i in range(0, len(others), 2)]
        mine = others[0]
    other = exchange(mine, SEQ, 2)
    mine = jnp.where(high == 0, jnp.concatenate([mine, other]), jnp.concatenate([other, mine]))
    other = exchange(mine, SEQ, 1)
    return jnp.where(low == 0, jnp.concatenate([mine, other]), jnp.concatenate([other, mine]))


def reorder(parts, mine):
    stacked = jnp.stack(parts)
    return [lax.dynamic_index_in_dim(stacked, mine ^ p, 0, keepdims=False) for p in range(GROUP)]


def mine_of(array, mine, axis):
    return lax.dynamic_index_in_dim(array, mine, axis, keepdims=False)


VMEM = pl.BlockSpec(memory_space=pltpu.VMEM)
SMEM = pl.BlockSpec(memory_space=pltpu.SMEM)
ROWS = (((0,), (0,)), ((), ()))
LAST = (((1,), (1,)), ((), ()))


def local_call(kernel, outs, inputs, scratch=()):
    return pl.pallas_call(
        kernel,
        out_shape=[jax.ShapeDtypeStruct(shape, kind) for shape, kind in outs],
        in_specs=[SMEM] + [VMEM] * (len(inputs) - 1),
        out_specs=[VMEM] * len(outs),
        scratch_shapes=list(scratch),
        compiler_params=pltpu.CompilerParams(vmem_limit_bytes=56 * 1024 * 1024),
    )(*inputs)


def pick(sources, blocks, outs, index):
    count = len(blocks)

    def kernel(index_ref, *refs):
        ins, results, sems = refs[: len(sources)], refs[len(sources) : -1], refs[-1]
        copies = []
        for number, (source, axis, start, out, there, length) in enumerate(blocks):
            begin = pl.multiple_of(start + index_ref[0] * length, length)
            if axis == 0:
                origin, target = ins[source].at[pl.ds(begin, length), :], results[out]
            else:
                origin = ins[source].at[:, pl.ds(begin, length)]
                target = results[out].at[:, pl.ds(there, length)]
            copies.append(pltpu.make_async_copy(origin, target, sems.at[number]))
        for copy in copies:
            copy.start()
        for copy in copies:
            copy.wait()

    return pl.pallas_call(
        kernel,
        out_shape=[jax.ShapeDtypeStruct(shape, bf16) for shape in outs],
        in_specs=[SMEM] + [pl.BlockSpec(memory_space=pl.ANY)] * len(sources),
        out_specs=[VMEM] * len(outs),
        scratch_shapes=[pltpu.SemaphoreType.DMA((count,))],
    )(index, *sources)


def place_in(index_ref, parts, out, source, target):
    rows = parts[0].shape[0]
    for j, part in enumerate(parts):
        at = pl.ds(pl.multiple_of(index_ref[j] * rows, rows), rows)
        out[at, target[0] : target[1]] = part[:, source[0] : source[1]]


def attention_forward(index, normed, firsts, seconds, query_bias, value_bias, segments):
    slots, width = normed.shape
    part = width // GROUP
    heads = part // HEAD_DIM
    rows = slots // GROUP
    count = len(firsts)
    scale = HEAD_DIM ** (-0.5)

    def kernel(index_ref, x_ref, *refs):
        halves, refs = (refs[:count], refs[count : 2 * count]), refs[2 * count :]
        qb_ref, vb_ref, seg_rows, seg_cols = refs[:4]
        w_out, q_out, k_out, v_out, att_out, total_out = refs[4:]
        place_in(index_ref, halves[0], w_out, (0, part), (0, part))
        place_in(index_ref, halves[1], w_out, (0, 2 * part), (part, 3 * part))
        projected = jnp.dot(x_ref[...], w_out[...], preferred_element_type=f32)
        queries = (projected[:, :part] + qb_ref[...]).astype(bf16)
        for block in range(GROUP):
            q_out[block] = queries[block * rows : (block + 1) * rows]
        k_out[...] = projected[:, part : 2 * part].astype(bf16)
        v_out[...] = (projected[:, 2 * part :] + vb_ref[...]).astype(bf16)

        def step(block, carry):
            same = seg_rows[block] == seg_cols[...]
            mixed, totals = [], []
            for h in range(heads):
                lanes = slice(h * HEAD_DIM, (h + 1) * HEAD_DIM)
                raw = lax.dot_general(
                    q_out[block, :, lanes], k_out[:, lanes], LAST, preferred_element_type=f32
                )
                logits = jnp.where(same, raw * scale, masked_value)
                top = jnp.max(logits, axis=-1, keepdims=True)
                raised = jnp.exp(logits - top)
                total = jnp.sum(raised, axis=-1, keepdims=True)
                probs = (raised * (1.0 / total)).astype(bf16)
                mixed.append(jnp.dot(probs, v_out[:, lanes], preferred_element_type=f32))
                totals.append(top + jnp.log(total))
            att_out[block] = jnp.concatenate(mixed, axis=1).astype(bf16)
            total_out[block] = jnp.concatenate(totals, axis=1)
            return carry

        lax.fori_loop(0, GROUP, step, 0)

    outs = [
        ((width, 3 * part), bf16),
        ((GROUP, rows, part), bf16),
        ((slots, part), bf16),
        ((slots, part), bf16),
        ((GROUP, rows, part), bf16),
        ((GROUP, rows, heads), f32),
    ]
    inputs = [index, normed, *firsts, *seconds, query_bias[None], value_bias[None]]
    inputs += [segments.reshape(GROUP, rows, 1), segments[None]]
    return local_call(kernel, outs, inputs)


def attention_backward(queries, keys, values, mixed_grad, totals, segments):
    blocks, rows, part = queries.shape
    slots = keys.shape[0]
    heads = part // HEAD_DIM
    scale = HEAD_DIM ** (-0.5)

    def kernel(zero_ref, q_ref, k_ref, v_ref, g_ref, t_ref, seg_rows, seg_cols, out, sums, acc):
        acc[...] = jnp.zeros_like(acc)

        def step(block, carry):
            same = seg_rows[block] == seg_cols[...]
            q_grads, k_grads, v_grads = [], [], []
            for h in range(heads):
                lanes = slice(h * HEAD_DIM, (h + 1) * HEAD_DIM)
                query, key, grad = q_ref[block, :, lanes], k_ref[:, lanes], g_ref[block, :, lanes]
                raw = lax.dot_general(query, key, LAST, preferred_element_type=f32)
                logits = jnp.where(same, raw * scale, masked_value)
                probs = jnp.exp(logits - t_ref[block, :, h : h + 1])
                probs_grad = lax.dot_general(
                    grad, v_ref[:, lanes], LAST, preferred_element_type=f32
                )
                weighted = probs * probs_grad
                inner = jnp.sum(weighted, axis=-1, keepdims=True)
                score = (scale * (weighted - probs * inner)).astype(bf16)
                q_grads.append(jnp.dot(score, key, preferred_element_type=f32))
                k_grads.append(
                    lax.dot_general(score, query, ROWS, preferred_element_type=f32)
                )
                v_grads.append(
                    lax.dot_general(probs.astype(bf16), grad, ROWS, preferred_element_type=f32)
                )
            start = pl.multiple_of(block * rows, 8)
            acc[pl.ds(start, rows), :part] = jnp.concatenate(q_grads, axis=1)
            acc[:, part:] += jnp.concatenate(k_grads + v_grads, axis=1)
            return carry

        lax.fori_loop(0, blocks, step, 0)
        rounded = acc[...].astype(bf16)
        out[...] = rounded
        sums[...] = jnp.sum(rounded.astype(f32), axis=0, keepdims=True)

    outs = [((slots, 3 * part), bf16), ((1, 3 * part), f32)]
    inputs = [jnp.zeros((1,), jnp.int32), queries, keys, values]
    inputs += [mixed_grad.reshape(blocks, rows, part), totals]
    inputs += [segments.reshape(blocks, rows, 1), segments[None]]
    scratch = [pltpu.VMEM((slots, 3 * part), f32)]
    return local_call(kernel, outs, inputs, scratch)


def feed_forward(index, seconds, parts, bias):
    rows, width = seconds[0].shape
    count, units = len(parts), parts[0].shape[1]
    half = 0.5**0.5

    def kernel(index_ref, *refs):
        xs, refs = refs[:GROUP], refs[GROUP:]
        weights, refs = refs[:count], refs[count:]
        b_ref, w_out, x_out, active_out, slope_out, upper = refs
        place_in(index_ref, weights, w_out, (0, units), (0, units))
        for j in range(GROUP):
            x_out[j] = xs[j][...]
            upper[...] = jnp.dot(xs[j][...], w_out[...], preferred_element_type=f32) + b_ref[...]

            def step(i, carry, j=j):
                at = pl.ds(pl.multiple_of(i * 8, 8), 8)
                u = upper[at, :]
                share = 0.5 * (1.0 + lax.erf(u * half))
                upper[at, :] = u * share
                slope_out[j, at, :] = share + u * jnp.exp(-0.5 * u * u) * 0.3989422804014327
                return carry

            lax.fori_loop(0, rows // 8, step, 0)
            active_out[j] = upper[...].astype(bf16)

    outs = [
        ((width, units), bf16),
        ((GROUP, rows, width), bf16),
        ((GROUP, rows, units), bf16),
        ((GROUP, rows, units), f32),
    ]
    inputs = [index, *seconds, *parts, bias[None]]
    return local_call(kernel, outs, inputs, [pltpu.VMEM((rows, units), f32)])


def feed_backward(index, upstream, parts, slope, up_full):
    blocks, rows, units = slope.shape
    width = upstream.shape[-1]
    count = len(parts)

    def kernel(index_ref, g_ref, *refs):
        weights, refs = refs[:count], refs[count:]
        s_ref, up_ref, w_out, upper_out, sums, sent, kept = refs
        place_in(index_ref, weights, w_out, (0, width), (0, width))
        for j in (3, 1, 2, 0):
            grad = lax.dot_general(g_ref[j], w_out[...], LAST, preferred_element_type=f32)
            low = (grad * s_ref[j]).astype(bf16)
            upper_out[j] = low
            total = jnp.sum(low.astype(f32), axis=0, keepdims=True)
            sums[...] = total if j == 3 else sums[...] + total
            back = lax.dot_general(low, up_ref[...], LAST, preferred_element_type=f32)
            if j % 2:
                sent[(3 - j) // 2] = back.astype(bf16)
            else:
                kept[(2 - j) // 2] = back

    outs = [
        ((count * parts[0].shape[0], width), bf16),
        ((blocks, rows, units), bf16),
        ((1, units), f32),
        ((2, rows, width), bf16),
        ((2, rows, width), f32),
    ]
    return local_call(kernel, outs, [index, upstream, *parts, slope, up_full])


def weight_pieces(index, left, right):
    count = index.shape[0]
    rows = left.shape[1] // count
    shape = (count // 2, rows, right.shape[1])

    def kernel(index_ref, left_ref, right_ref, sent, kept):
        for j in [*range(1, count, 2), *range(0, count, 2)]:
            block = left_ref[:, pl.ds(pl.multiple_of(index_ref[j] * rows, rows), rows)]
            term = lax.dot_general(block, right_ref[...], ROWS, preferred_element_type=f32)
            if j % 2:
                sent[j // 2] = term.astype(bf16)
            else:
                kept[j // 2] = term

    return local_call(kernel, [(shape, bf16), (shape, f32)], [index, left, right])


def group_terms(owners, left, right):
    columns = right.shape[1] // GROUP

    def kernel(owner_ref, left_ref, right_ref, *outs):
        for j in range(GROUP):
            start = pl.multiple_of(owner_ref[j] * columns, columns)
            block = right_ref[:, pl.ds(start, columns)]
            term = lax.dot_general(left_ref[...], block, ROWS, preferred_element_type=f32)
            outs[j][...] = term.astype(bf16)

    shape = ((left.shape[1], columns), bf16)
    return local_call(kernel, [shape] * GROUP, [owners, left, right])


def fold(kept, received):
    count, rows, columns = kept.shape

    def kernel(zero_ref, kept_ref, received_ref, own, *sent):
        for digit in range(1, count):
            sent[digit - 1][...] = (kept_ref[digit] + received_ref[digit].astype(f32)).astype(bf16)
        own[...] = kept_ref[0] + received_ref[0].astype(f32)

    outs = [((rows, columns), f32)] + [((rows, columns), bf16)] * (count - 1)
    return local_call(kernel, outs, [jnp.zeros((1,), jnp.int32), kept, received])


def finish(groups):
    sizes = [len(group) for group in groups]
    widths = [group[0].shape[1] for group in groups]
    rows = groups[0][0].shape[0]

    def kernel(zero_ref, *refs):
        refs, out = refs[:-1], refs[-1]
        start = column = 0
        for size, columns in zip(sizes, widths):
            total = refs[start][...]
            for other in refs[start + 1 : start + size]:
                total = total + other[...].astype(f32)
            out[:, column : column + columns] = total.astype(bf16)
            start, column = start + size, column + columns

    inputs = [jnp.zeros((1,), jnp.int32)] + [value for group in groups for value in group]
    return local_call(kernel, [((rows, sum(widths)), bf16)], inputs)[0]


def scatter_pieces(pieces):
    sent, kept = pieces
    own, *others = fold(kept, exchange(sent, IMG, 1))
    return [own] + [exchange(other, IMG, 2 * digit) for digit, other in enumerate(others, 1)]


def row_halves(left, right, transposed):
    _, rows = left.shape[:2]
    columns = right.shape[0 if transposed else 1]
    dims = LAST if transposed else (((1,), (0,)), ((), ()))

    def kernel(zero_ref, left_ref, right_ref, sent, kept):
        for j in (3, 1, 2, 0):
            value = lax.dot_general(left_ref[j], right_ref[...], dims, preferred_element_type=f32)
            if j % 2:
                sent[(3 - j) // 2] = value.astype(bf16)
            else:
                kept[(2 - j) // 2] = value

    outs = [((2, rows, columns), bf16), ((2, rows, columns), f32)]
    return local_call(kernel, outs, [jnp.zeros((1,), jnp.int32), left, right])


def add_far(kept, beside):
    def kernel(zero_ref, kept_ref, beside_ref, out):
        out[...] = (kept_ref[0] + beside_ref[0].astype(f32)).astype(bf16)

    inputs = [jnp.zeros((1,), jnp.int32), kept, beside]
    return local_call(kernel, [(kept.shape[1:], bf16)], inputs)[0]


def block_end(kept, beside, moved, hidden, bias, valid):
    def kernel(zero_ref, kept_ref, beside_ref, moved_ref, hidden_ref, bias_ref, valid_ref, out):
        branch = kept_ref[1] + beside_ref[1].astype(f32) + moved_ref[...].astype(f32)
        value = hidden_ref[...] + branch + bias_ref[...]
        out[...] = jnp.where(valid_ref[...] > 0, value, 0.0).astype(bf16)

    inputs = [jnp.zeros((1,), jnp.int32), kept, beside, moved, hidden, bias[None]]
    inputs.append(valid[:, None].astype(f32))
    return local_call(kernel, [(hidden.shape, bf16)], inputs)[0]


def output_places(index, seq_vector, parts):
    rows, columns = parts[0].shape
    size = columns // 2
    per_group = len(parts) // GROUP

    def kernel(index_ref, seq_ref, *refs):
        out = refs[-1]
        for j in range(len(parts)):
            group, place = index_ref[j] // per_group, index_ref[j] % per_group
            at = pl.ds(pl.multiple_of(place * rows, rows), rows)
            out[group ^ seq_ref[0], at, :] = refs[j][:, size:]

    return pl.pallas_call(
        kernel,
        out_shape=jax.ShapeDtypeStruct((GROUP, per_group * rows, size), bf16),
        in_specs=[SMEM, SMEM] + [VMEM] * len(parts),
        out_specs=VMEM,
    )(index, seq_vector, *parts)


def branch_halves(owners, attended, blocks):
    _, rows, part = attended.shape
    width = part * GROUP

    def kernel(owner_ref, a_ref, *refs):
        parts, (w_out, sent, kept) = refs[:GROUP], refs[GROUP:]
        for k in range(GROUP):
            w_out[:, pl.ds(pl.multiple_of(owner_ref[k] * part, part), part)] = parts[k][...]
        for j in (3, 1, 2, 0):
            value = jnp.dot(a_ref[j], w_out[...], preferred_element_type=f32)
            if j % 2:
                sent[(3 - j) // 2] = value.astype(bf16)
            else:
                kept[(2 - j) // 2] = value

    outs = [((part, width), bf16), ((2, rows, width), bf16), ((2, rows, width), f32)]
    return local_call(kernel, outs, [owners, attended, *blocks])


def spread_columns(owners, parts, repeats):
    rows, total = parts[0].shape
    size = total // sum(repeats)

    def kernel(owner_ref, *refs):
        for j in range(GROUP):
            column = 0
            for out, count in zip(refs[GROUP:], repeats):
                for r in range(count):
                    start = pl.multiple_of((r * GROUP + owner_ref[j]) * size, size)
                    out[:, pl.ds(start, size)] = refs[j][:, column : column + size].astype(f32)
                    column += size

    outs = [((rows, count * GROUP * size), f32) for count in repeats]
    return local_call(kernel, outs, [owners, *parts])


def spread_rows(owners, parts):
    rows, columns = parts[0].shape

    def kernel(owner_ref, *refs):
        for j in range(GROUP):
            start = pl.multiple_of(owner_ref[j] * rows, rows)
            refs[GROUP][pl.ds(start, rows), :] = refs[j][...].astype(f32)

    return local_call(kernel, [((rows * GROUP, columns), f32)], [owners, *parts])[0]


def generic_device(
    tokens,
    classes,
    source_index,
    position_table,
    input_weight,
    query_bias,
    value_bias,
    output_weight,
    output_bias,
    up_weight,
    up_bias,
    down_weight,
    down_bias,
    first_gain,
    first_shift,
    second_gain,
    second_shift,
    cotangent,
):
    shard_rows, width = tokens.shape
    group_slots = shard_rows * GROUP
    size = lax.axis_size(IMG)
    img, seq = lax.axis_index(IMG), lax.axis_index(SEQ)
    held = width // size
    part = width // GROUP
    heads = HEADS // GROUP
    hidden_units = up_weight.shape[1]
    units = hidden_units // size // GROUP
    scale = HEAD_DIM ** (-0.5)

    input_part = mine_of(input_weight.reshape(held, 3, GROUP, part), seq, 2).reshape(held, 3 * part)
    output_part = mine_of(output_weight.reshape(held, GROUP, part), seq, 1)
    up_part = mine_of(up_weight.reshape(held, size, GROUP, units), seq, 2).reshape(held, size * units)
    down_part = mine_of(down_weight.reshape(GROUP, units, width), seq, 0)
    input_full = place(gather_relative(input_part), img).reshape(width, 3 * part)
    output_cols = place(gather_relative(output_part), img).reshape(GROUP, part, part)
    up_full = place(gather_relative(up_part), img).reshape(width, size * units)
    down_full = place(gather_relative(down_part), img).reshape(size * units, width)
    output_blocks = [mine_of(output_cols, seq, 0)] + [
        exchange(mine_of(output_cols, seq ^ j, 0), SEQ, j) for j in range(1, GROUP)
    ]
    output_full = jnp.concatenate(reorder(output_blocks, seq), axis=1)
    query_bias_part = mine_of(query_bias.reshape(GROUP, part), seq, 0)
    value_bias_part = mine_of(value_bias.reshape(GROUP, part), seq, 0)
    up_bias_part = mine_of(up_bias.reshape(size, GROUP, units), seq, 1).reshape(size * units)

    my_slots = seq * shard_rows + jnp.arange(shard_rows, dtype=jnp.int32)
    _, valid, mixing = table_mixing(classes, my_slots, source_index)
    owners = seq ^ jnp.arange(GROUP, dtype=jnp.int32)
    all_slots = (owners[:, None] * shard_rows + jnp.arange(shard_rows, dtype=jnp.int32)[None]).reshape(-1)
    all_segments, _ = slot_segments(classes, all_slots)
    same_image = all_segments[:, None] == all_segments[None, :]

    upstream = jnp.where(valid[:, None], cotangent.astype(f32), 0.0)
    upstream_all = jnp.concatenate(group_gather(upstream.astype(bf16)), axis=0)

    embedded = tokens.astype(f32) + jnp.dot(mixing, position_table, precision=highest)
    first_value, first_pull = jax.vjp(layer_norm, embedded, first_gain, first_shift)
    normed_all = jnp.concatenate(group_gather(first_value.astype(bf16)), axis=0)
    projected = jnp.dot(normed_all, input_full, preferred_element_type=f32)

    def split_heads(value):
        return value.astype(bf16).reshape(group_slots, heads, HEAD_DIM)

    queries = split_heads(projected[:, :part] + query_bias_part)
    keys = split_heads(projected[:, part : 2 * part])
    values = split_heads(projected[:, 2 * part :] + value_bias_part)
    raw_scores = jnp.einsum("qhd,khd->hqk", queries, keys, preferred_element_type=f32)
    logits = jnp.where(same_image[None], raw_scores * scale, masked_value)
    row_max = jnp.max(logits, axis=-1, keepdims=True)
    log_total = row_max + jnp.log(jnp.sum(jnp.exp(logits - row_max), axis=-1, keepdims=True))
    probs = jnp.exp(logits - log_total)
    probs_low = probs.astype(bf16)
    attended = (
        jnp.einsum("hqk,khd->qhd", probs_low, values, preferred_element_type=f32)
        .reshape(group_slots, part)
        .astype(bf16)
    )

    def row_parts(value):
        return [value[j * shard_rows : (j + 1) * shard_rows] for j in range(GROUP)]

    branch_one = group_scatter(row_parts(jnp.dot(attended, output_full, preferred_element_type=f32)))
    hidden = embedded + branch_one + output_bias
    second_value, second_pull = jax.vjp(layer_norm, hidden, second_gain, second_shift)
    second_all = jnp.concatenate(group_gather(second_value.astype(bf16)), axis=0)
    upper = jnp.dot(second_all, up_full, preferred_element_type=f32) + up_bias_part
    active, gelu_pull = jax.vjp(exact_gelu, upper)
    active_low = active.astype(bf16)

    def to_owners(term, rows):
        pieces = term.reshape(size, rows, term.shape[1])
        return scatter_relative([mine_of(pieces, img ^ j, 0) for j in range(size)])

    def columns_of_all(total):
        return reorder(group_gather(total.astype(bf16)), seq)

    down_sum = to_owners(
        jnp.einsum("sf,sd->fd", active_low, upstream_all, preferred_element_type=f32), units
    )
    active_grad = jnp.einsum("sd,fd->sf", upstream_all, down_full, preferred_element_type=f32)
    upper_low = gelu_pull(active_grad)[0].astype(bf16)
    second_grad = group_scatter(
        row_parts(jnp.einsum("sf,df->sd", upper_low, up_full, preferred_element_type=f32))
    )
    up_sum = to_owners(
        jnp.einsum("sd,sf->df", second_all, upper_low, preferred_element_type=f32), held
    )
    branch_two = group_scatter(row_parts(jnp.dot(active_low, down_full, preferred_element_type=f32)))
    block_out = jnp.where(valid[:, None], hidden + branch_two + down_bias, 0.0).astype(bf16)

    hidden_grad, second_gain_grad, second_shift_grad = second_pull(second_grad)
    hidden_grad = hidden_grad + upstream
    branch_low = hidden_grad.astype(bf16)
    branch_all = jnp.concatenate(group_gather(branch_low), axis=0)
    output_term = jnp.einsum("sc,sd->cd", attended, branch_all, preferred_element_type=f32)
    output_term = output_term.astype(bf16).reshape(part, GROUP, part)
    term_blocks = [mine_of(output_term, seq, 1)] + [
        exchange(mine_of(output_term, seq ^ j, 1), SEQ, j) for j in range(1, GROUP)
    ]
    output_sum = to_owners(jnp.concatenate(reorder(term_blocks, seq), axis=0).astype(f32), held)

    attended_grad = jnp.einsum(
        "sd,cd->sc", branch_all, output_full, preferred_element_type=f32
    )
    attended_grad = split_heads(attended_grad)
    probs_grad = jnp.einsum("qhd,khd->hqk", attended_grad, values, preferred_element_type=f32)
    inner = jnp.sum(probs * probs_grad, axis=-1, keepdims=True)
    score_low = (scale * (probs * (probs_grad - inner))).astype(bf16)
    query_grad = jnp.einsum("hqk,khd->qhd", score_low, keys, preferred_element_type=f32)
    key_grad = jnp.einsum("hqk,qhd->khd", score_low, queries, preferred_element_type=f32)
    value_grad = jnp.einsum("hqk,qhd->khd", probs_low, attended_grad, preferred_element_type=f32)
    projection_grad = jnp.concatenate(
        [grad.reshape(group_slots, part).astype(bf16) for grad in (query_grad, key_grad, value_grad)],
        axis=1,
    )
    input_sum = to_owners(
        jnp.einsum("sd,se->de", normed_all, projection_grad, preferred_element_type=f32), held
    )
    normed_grad = group_scatter(
        row_parts(jnp.einsum("se,de->sd", projection_grad, input_full, preferred_element_type=f32))
    )
    embedded_grad, first_gain_grad, first_shift_grad = first_pull(normed_grad)
    embedded_grad = embedded_grad + hidden_grad
    table_term = jnp.einsum("st,sd->td", mixing, embedded_grad, precision=highest)

    input_columns = [c.reshape(held, 3, part) for c in columns_of_all(input_sum)]
    input_weight_grad = jnp.stack(input_columns, axis=2).reshape(held, 3 * width).astype(f32)
    output_weight_grad = jnp.concatenate(columns_of_all(output_sum), axis=1).astype(f32)
    up_columns = [c.reshape(held, size, units) for c in columns_of_all(up_sum)]
    up_weight_grad = jnp.stack(up_columns, axis=2).reshape(held, hidden_units).astype(f32)
    down_weight_grad = jnp.concatenate(columns_of_all(down_sum), axis=0).astype(f32)

    def spread(value, shape, axis):
        value = jnp.expand_dims(value.reshape(shape), axis)
        mask = jnp.arange(GROUP, dtype=jnp.int32).reshape([-1 if a == axis else 1 for a in range(value.ndim)])
        return jnp.where(mask == seq, value, 0.0).reshape(-1)

    def columns(value):
        return jnp.sum(value.astype(f32), axis=0)

    projection_sums = columns(projection_grad)
    rows = [
        table_term,
        spread(projection_sums[:part], (part,), 0),
        spread(projection_sums[2 * part :], (part,), 0),
        columns(branch_low),
        columns(upstream),
        first_gain_grad,
        first_shift_grad,
        second_gain_grad,
        second_shift_grad,
        spread(columns(upper_low), (size, units), 1),
    ]
    packed = jnp.concatenate([row.reshape(-1, width) for row in rows])
    used = packed.shape[0]
    packed = jnp.pad(packed, ((0, -used % 32), (0, 0)))
    total = sum_everywhere(packed)
    vectors = total[TABLE:used]
    return (
        block_out,
        embedded_grad.astype(bf16),
        total[:TABLE],
        input_weight_grad,
        vectors[0],
        vectors[1],
        output_weight_grad,
        vectors[2],
        up_weight_grad,
        vectors[8:].reshape(-1),
        down_weight_grad,
        vectors[3],
        vectors[4],
        vectors[5],
        vectors[6],
        vectors[7],
    )


def on_device(
    tokens,
    classes,
    source_index,
    position_table,
    input_weight,
    query_bias,
    value_bias,
    output_weight,
    output_bias,
    up_weight,
    up_bias,
    down_weight,
    down_bias,
    first_gain,
    first_shift,
    second_gain,
    second_shift,
    cotangent,
):
    if up_weight.shape[1] // lax.axis_size(IMG) // GROUP % 128:
        return generic_device(
            tokens,
            classes,
            source_index,
            position_table,
            input_weight,
            query_bias,
            value_bias,
            output_weight,
            output_bias,
            up_weight,
            up_bias,
            down_weight,
            down_bias,
            first_gain,
            first_shift,
            second_gain,
            second_shift,
            cotangent,
        )
    shard_rows, width = tokens.shape
    size = lax.axis_size(IMG)
    img, seq = lax.axis_index(IMG), lax.axis_index(SEQ)
    held = width // size
    part = width // GROUP
    hidden_units = up_weight.shape[1]
    units = hidden_units // size // GROUP
    relatives = img ^ jnp.arange(size, dtype=jnp.int32)
    owners = seq ^ jnp.arange(GROUP, dtype=jnp.int32)
    seq_vector = seq[None].astype(jnp.int32)

    blocks = [(0, 1, t * width, 1, (t - 1) * part, part) for t in (1, 2)]
    blocks += [(0, 1, 0, 0, 0, part), (1, 1, 0, 0, part, part)]
    first_part, second_part = pick(
        [input_weight, output_weight], blocks, [(held, 2 * part)] * 2, seq_vector
    )
    first_parts = gather_relative(first_part)
    second_parts = gather_relative(second_part)
    blocks = [(0, 1, i * GROUP * units, 0, i * units, units) for i in range(size)]
    up_part, down_part = pick(
        [up_weight, down_weight],
        blocks + [(1, 0, 0, 1, 0, units)],
        [(held, size * units), (units, width)],
        seq_vector,
    )
    up_parts = gather_relative(up_part)
    down_parts = gather_relative(down_part)

    query_bias_part = mine_of(query_bias.reshape(GROUP, part), seq, 0)
    value_bias_part = mine_of(value_bias.reshape(GROUP, part), seq, 0)
    up_bias_part = mine_of(up_bias.reshape(size, GROUP, units), seq, 1).reshape(size * units)

    my_slots = seq * shard_rows + jnp.arange(shard_rows, dtype=jnp.int32)
    _, valid, mixing = table_mixing(classes, my_slots, source_index)
    all_slots = owners[:, None] * shard_rows + jnp.arange(shard_rows, dtype=jnp.int32)[None]
    all_segments, _ = slot_segments(classes, all_slots.reshape(-1))

    embedded = tokens.astype(f32) + jnp.dot(mixing, position_table, precision=highest)
    first_value, first_pull = jax.vjp(layer_norm, embedded, first_gain, first_shift)
    normed_all = jnp.concatenate(group_gather(first_value.astype(bf16)), axis=0)
    upstream = jnp.where(valid[:, None], cotangent.astype(f32), 0.0)
    upstream_all = jnp.concatenate(group_gather(upstream.astype(bf16)), axis=0)

    columns_of = output_places(relatives, seq_vector, first_parts)
    output_blocks = [columns_of[0]] + [exchange(columns_of[j], SEQ, j) for j in range(1, GROUP)]
    input_full, queries, keys, values, attended, totals = attention_forward(
        relatives, normed_all, first_parts, second_parts, query_bias_part, value_bias_part, all_segments
    )
    output_full, sent, kept = branch_halves(owners, attended, output_blocks)
    attended = attended.reshape(GROUP * shard_rows, part)
    branch_one = group_total(sent, kept)
    hidden = embedded + branch_one + output_bias
    second_value, second_pull = jax.vjp(layer_norm, hidden, second_gain, second_shift)
    second_rows = group_gather(second_value.astype(bf16))
    up_full, second_all, active, slope = feed_forward(relatives, second_rows, up_parts, up_bias_part)
    second_all = second_all.reshape(GROUP * shard_rows, width)
    flat_active = active.reshape(GROUP * shard_rows, size * units)
    down_sum = scatter_pieces(weight_pieces(relatives, flat_active, upstream_all))
    down_full, upper_low, upper_sums, sent, kept = feed_backward(
        relatives, upstream_all.reshape(GROUP, shard_rows, width), down_parts, slope, up_full
    )
    upper_low = upper_low.reshape(GROUP * shard_rows, size * units)
    second_grad = group_total(sent, kept)
    up_sum = scatter_pieces(weight_pieces(relatives, second_all, upper_low))
    sent, kept = row_halves(active, down_full, False)
    beside = exchange(sent, SEQ, 1)
    far = add_far(kept, beside)
    moved = exchange(far, SEQ, 2)
    block_out = block_end(kept, beside, moved, hidden, down_bias, valid)

    hidden_grad, second_gain_grad, second_shift_grad = second_pull(second_grad)
    hidden_grad = hidden_grad + upstream
    branch_low = hidden_grad.astype(bf16)
    branch_all = jnp.concatenate(group_gather(branch_low), axis=0)
    mixed_grad = jnp.einsum("sd,cd->sc", branch_all, output_full, preferred_element_type=f32)
    projection_grad, projection_sums = attention_backward(
        queries, keys, values, mixed_grad.astype(bf16), totals, all_segments
    )
    projection_sums = projection_sums[0]

    term_blocks = group_terms(owners, attended, branch_all)
    term_blocks = [term_blocks[0]] + [exchange(term_blocks[j], SEQ, j) for j in range(1, GROUP)]
    per_group = size // GROUP
    stacked = jnp.stack(term_blocks).reshape(size, held, part)
    pieces = [
        mine_of(stacked, ((img ^ j) // per_group ^ seq) * per_group + (img ^ j) % per_group, 0)
        for j in range(size)
    ]
    output_sum = scatter_pieces((jnp.stack(pieces[1::2]), jnp.stack(pieces[0::2]).astype(f32)))
    input_sum = scatter_pieces(weight_pieces(relatives, normed_all, projection_grad))
    row_grads = projection_grad.reshape(GROUP, shard_rows, 3 * part)
    normed_grad = group_total(*row_halves(row_grads, input_full, True))
    embedded_grad, first_gain_grad, first_shift_grad = first_pull(normed_grad)
    embedded_grad = embedded_grad + hidden_grad
    table_term = jnp.einsum("st,sd->td", mixing, embedded_grad, precision=highest)

    up_shares = group_gather(finish([up_sum]))
    down_shares = group_gather(finish([down_sum]))
    last_shares = group_gather(finish([input_sum, output_sum]))
    up_weight_grad = spread_columns(owners, up_shares, [size])[0]
    down_weight_grad = spread_rows(owners, down_shares)
    input_weight_grad, output_weight_grad = spread_columns(owners, last_shares, [3, 1])

    def spread(value, shape, axis):
        value = jnp.expand_dims(value.reshape(shape), axis)
        mask = jnp.arange(GROUP, dtype=jnp.int32).reshape([-1 if a == axis else 1 for a in range(value.ndim)])
        return jnp.where(mask == seq, value, 0.0).reshape(-1)

    def columns(value):
        return jnp.sum(value.astype(f32), axis=0)

    rows = [
        table_term,
        spread(projection_sums[:part], (part,), 0),
        spread(projection_sums[2 * part :], (part,), 0),
        columns(branch_low),
        columns(upstream),
        first_gain_grad,
        first_shift_grad,
        second_gain_grad,
        second_shift_grad,
        spread(upper_sums[0], (size, units), 1),
    ]
    packed = jnp.concatenate([row.reshape(-1, width) for row in rows])
    used = packed.shape[0]
    packed = jnp.pad(packed, ((0, -used % 32), (0, 0)))
    total = sum_everywhere(packed)
    vectors = total[TABLE:used]
    return (
        block_out,
        embedded_grad.astype(bf16),
        total[:TABLE],
        input_weight_grad,
        vectors[0],
        vectors[1],
        output_weight_grad,
        vectors[2],
        up_weight_grad,
        vectors[8:].reshape(-1),
        down_weight_grad,
        vectors[3],
        vectors[4],
        vectors[5],
        vectors[6],
        vectors[7],
    )


def solution(mesh):
    placed = (
        P((IMG, SEQ), None),
        P(IMG),
        P(),
        P(),
        P(IMG, None),
        P(),
        P(),
        P(IMG, None),
        P(),
        P(IMG, None),
        P(),
        P(IMG, None),
        P(),
        P(),
        P(),
        P(),
        P(),
        P((IMG, SEQ), None),
    )
    return jax.shard_map(
        on_device,
        mesh=mesh,
        in_specs=placed,
        out_specs=(
            P((IMG, SEQ), None),
            P((IMG, SEQ), None),
            P(),
            P(IMG, None),
            P(),
            P(),
            P(IMG, None),
            P(),
            P(IMG, None),
            P(),
            P(IMG, None),
            P(),
            P(),
            P(),
            P(),
            P(),
        ),
        check_vma=False,
    )
```
